1024 devices in a mesh: energy: 16 (over z), slab: 64 (over y, x, core).
Axes of the slice: x: 4, y: 8, z: 16, core: 2. Of those that a mesh axis runs over, the one named last changes fastest.
Arguments:
- hamiltonian: float32 [16384, 256], P('slab'), as said below
- decay: float32 [64, 256], P('slab'), may hold values from 0 to 1, as said below
- coupling: float32 [64, 256], P('slab'), may hold values from 0.2 to 2
- rows: int32 [64, 32], P('slab'), may hold values from 0 to 255
- screened: float32 [64, 128, 32, 256], P('slab', None, 'energy'), may hold values from -0.5 to 0.5
Outputs:
- sigma: float32 [128, 2048, 256], P('energy', 'slab')
The draws below stay inside these ranges and needn't reach their ends.
Inputs may be any that keep to these rules, and one draw needn't show every extreme that they name: `hamiltonian`: entries are independent and small enough that every H_s / z_k has spectral radius well under one. `decay`: every entry lies strictly between 0 and 1.
All inputs are finite; a program needn't handle non-finite values.
Results may differ from the reference program's by a relative error of at most 0.0001.
Values sent between devices are 32-bit elements; how exact they have to be, the bound alone decides.
No kernel may reach another device: no remote copies, remote signals or barrier semaphores. Data moves between devices by JAX's collectives and lax.ppermute only.
A program may use at most 128 MiB of HBM per device.

```python
import math
import jax
import jax.numpy as jnp
from jax import lax

BS = 256
NR = 32
NS_ITERS = 2
LAYER_NUMBER = 64
NE = 128


def draw_hamiltonian(key, part):
    extent = (LAYER_NUMBER * BS, BS)
    deviation = 1.0 / (3.0 * math.sqrt(BS))
    values = jnp.clip(jax.random.normal(key, extent, jnp.float32), -3.0, 3.0) * deviation
    return values


def draw_decay(key, part):
    keys = jax.random.split(key, 6)
    fraction_share = 0.5
    lasting = jax.random.uniform(keys[0], (BS,), jnp.float32) < fraction_share
    slow_rate = jax.random.uniform(keys[1], (BS,), jnp.float32, 0.1, 0.5) / LAYER_NUMBER
    fast_rate = jax.random.uniform(keys[2], (BS,), jnp.float32, 1.0, 3.0)
    rates_base = jnp.where(lasting, slow_rate, fast_rate)
    variation = jax.random.uniform(keys[3], (LAYER_NUMBER, BS), jnp.float32, 0.6, 1.6)
    density_averages = jax.random.randint(keys[4], (2,), 0, LAYER_NUMBER)
    packet_batches = jnp.any(jnp.arange(LAYER_NUMBER)[:, None] == density_averages[None, :], axis=1)
    broadening_parts = jax.random.uniform(keys[5], (LAYER_NUMBER, BS), jnp.float32, 0.5, 0.8)
    scaling_factors = jnp.where(packet_batches[:, None], broadening_parts, 1.0)
    return jnp.exp(-rates_base[None, :] * variation) * scaling_factors


def place_ends(drawn, own_key, smallest, largest):
    place = [jax.random.randint(jax.random.fold_in(own_key, axis), (), 0, length) for axis, length in enumerate(drawn.shape)]
    longest = drawn.shape.index(max(drawn.shape))
    neighbour = place[:longest] + [(place[longest] + 1) % drawn.shape[longest]] + place[longest + 1:]
    return drawn.at[tuple(place)].set(smallest).at[tuple(neighbour)].set(largest)


def level_of(key, shape, shards, least, top_value):
    loudness = 1.0
    for dim, blocks in shards:
        steps = jax.random.uniform(jax.random.fold_in(jax.random.fold_in(key, 6), dim), (blocks,), jnp.float32, least / len(shards), top_value / len(shards))
        loudness = loudness * jnp.repeat(jnp.exp(steps), shape[dim] // blocks).reshape((-1,) + (1,) * (len(shape) - 1 - dim))
    return loudness


def scatter_about(key, shape, scale, reach, shards=(), held_as=jnp.bfloat16):
    result = jax.random.normal(key, shape, jnp.float32) * scale
    if len(shards) > 0:
        result = level_of(key, shape, shards, -0.22, 0.18) * result
    return jnp.clip(result, min=-reach, max=reach).astype(held_as)


def setup_inputs(seed: int = 0) -> dict:
    arg_keys = jax.random.split(jax.random.key(seed), 6)
    hamiltonian = draw_hamiltonian(jax.random.fold_in(arg_keys[5], 71), 0)
    decay = draw_decay(jax.random.fold_in(arg_keys[5], 71), 0)
    coupling = jnp.clip(jnp.exp(math.log(2.0) - 2.3025851 * jax.random.uniform(arg_keys[2], (LAYER_NUMBER, BS), jnp.float32) ** level_of(arg_keys[2], (LAYER_NUMBER, BS), ((0, 64),), -0.2, 0.2)), 0.2, 2.0)
    rows = place_ends(jax.random.randint(arg_keys[3], (LAYER_NUMBER, NR), 0, BS), jax.random.fold_in(arg_keys[3], 1), 0, BS - 1).astype(jnp.int32)
    screened = scatter_about(arg_keys[4], (LAYER_NUMBER, NE, NR, BS), NE ** -0.5, 0.5, ((0, 64), (2, 16)), jnp.float32)
    return dict(hamiltonian=hamiltonian, decay=decay, coupling=coupling, rows=rows, screened=screened)


FULL_PRECISION = lax.Precision.HIGHEST


def local_green(hamilton_block, shifts):
    identity = jnp.eye(hamilton_block.shape[0], dtype=jnp.float32)
    column = shifts[:, None, None]
    green_block = (identity[None] + hamilton_block[None] / column) / column
    for sweep_index in range(NS_ITERS):
        applied = jnp.einsum("ij,kjl->kil", hamilton_block, green_block, precision=FULL_PRECISION)
        shifted = column * green_block - applied
        green_block = 2.0 * green_block - jnp.einsum("kij,kjl->kil", green_block, shifted, precision=FULL_PRECISION)
    return green_block


def reference(hamiltonian, decay, coupling, rows, screened):
    shifts = 1.0 + jnp.arange(NE, dtype=jnp.float32) / NE
    hamilton_blocks = hamiltonian.reshape(LAYER_NUMBER, BS, BS)

    def diagonals(hamilton_block):
        return jnp.diagonal(local_green(hamilton_block, shifts), axis1=1, axis2=2)

    diag_all = lax.map(diagonals, hamilton_blocks)
    injection_contributions = coupling[:, None, :] * diag_all / LAYER_NUMBER

    def advance(carried, inputs):
        decay_row, source_row = inputs
        return decay_row[None, :] * carried + source_row, carried

    _, incoming = lax.scan(advance, jnp.zeros((NE, BS), jnp.float32), (decay, injection_contributions))

    def slab_sigma(inputs):
        hamilton_block, entering, chosen, interaction = inputs
        green_block = local_green(hamilton_block, shifts)
        picked = jnp.take(green_block, chosen, axis=1)
        dressed = picked + jnp.einsum("kri,kij->krj", picked * entering[:, None, :], green_block, precision=FULL_PRECISION)
        product = jnp.fft.fft(dressed, axis=0) * jnp.fft.fft(interaction, axis=0)
        return jnp.real(jnp.fft.ifft(product, axis=0)).astype(jnp.float32)

    sigma_all = lax.map(slab_sigma, (hamilton_blocks, incoming, rows, screened))
    return jnp.transpose(sigma_all, (1, 0, 2, 3)).reshape(NE, LAYER_NUMBER * NR, BS)
```

```python
import math

import jax
import jax.numpy as jnp
import numpy as np
from jax import lax
from jax.experimental import pallas as pl
from jax.experimental.pallas import tpu as pltpu
from jax.sharding import Mesh
from jax.sharding import PartitionSpec as P

BS = 256
NE = 128
SLABS = 64
LANES = 128
TERMS = 8
FIELDS = TERMS + 1
VMEM_LIMIT = 48 * 1024 * 1024
HIGHEST = lax.Precision.HIGHEST


def tables():
    k = np.arange(NE)
    zeta = np.broadcast_to((1.0 / (1.0 + k / NE))[:, None], (NE, LANES))
    half = NE // 2
    angle = 2.0 * math.pi / NE * (np.arange(half)[:, None] * k[None, :] % NE)
    cosine, sine = np.cos(angle), np.sin(angle)
    sine[0] = (-1.0) ** k
    weight = np.full((half, 1), 2.0)
    weight[0] = 1.0
    forward = np.concatenate([cosine, sine], axis=0)
    inverse = np.concatenate([cosine * weight, sine * weight], axis=0).T / NE
    return tuple(np.ascontiguousarray(t, dtype=np.float32) for t in (zeta, forward, inverse))


def dot(a, b):
    return jnp.dot(a, b, precision=HIGHEST, preferred_element_type=jnp.float32)


def powers_kernel(h_ref, decay_ref, coupling_ref, own_ref, h2_ref, h4_ref):
    h = h_ref[...]
    ht = h.T
    h2 = dot(h, h)
    h2t = dot(ht, ht)
    h4 = dot(h2, h2)
    h3t = dot(h2t, ht)
    h2_ref[...] = h2
    h4_ref[...] = h4
    row = lax.broadcasted_iota(jnp.int32, (BS, BS), 0)
    column = lax.broadcasted_iota(jnp.int32, (BS, BS), 1)
    share = coupling_ref[...] * (1.0 / SLABS)
    fields = [decay_ref[...], share]
    for product in (
        jnp.where(row == column, h, 0.0),
        h * ht,
        h2 * ht,
        h2 * h2t,
        h4 * ht,
        h4 * h2t,
        h4 * h3t,
    ):
        fields.append(share * jnp.sum(product, axis=0, keepdims=True))
    for q, field in enumerate(fields):
        for half in range(2):
            own_ref[half : half + 1, q * LANES : (q + 1) * LANES] = field[
                :, half * LANES : (half + 1) * LANES
            ]


def picked_kernel(place_ref, rows_ref, h_ref, h2_ref, h4_ref, zeta_ref, screen_ref, forward_ref, picked_ref, hat_ref):
    first = place_ref[0] * 2
    column = lax.broadcasted_iota(jnp.int32, (1, BS), 1)
    z = zeta_ref[...]
    zeta = jnp.concatenate([z, z], axis=1)
    v0, v1, v2, v4 = [], [], [], []
    for r in range(2):
        row = rows_ref[first + r]
        v0.append(jnp.where(column == row, 1.0, 0.0))
        v1.append(h_ref[pl.ds(row, 1), :])
        v2.append(h2_ref[pl.ds(row, 1), :])
        v4.append(h4_ref[pl.ds(row, 1), :])
    blank = jnp.zeros((6, BS), jnp.float32)
    v3 = dot(jnp.concatenate([*v1, blank], axis=0), h2_ref[...])
    late = dot(jnp.concatenate([*v1, *v2, v3[:2], blank[:2]], axis=0), h4_ref[...])
    for r in range(2):
        series = [v0[r], v1[r], v2[r], v3[r : r + 1], v4[r]]
        series += [late[2 * j + r : 2 * j + r + 1] for j in range(3)]
        acc = jnp.broadcast_to(series[7], (NE, BS))
        for term in reversed(series[:7]):
            acc = term + zeta * acc
        picked_ref[r * NE : (r + 1) * NE, :] = zeta * acc
    hat_ref[...] = dot(forward_ref[...], screen_ref[...])


def compose_kernel(place_ref, own_ref, sibling_ref, out_ref):
    odd = place_ref[2] == 1
    own, sibling = own_ref[...], sibling_ref[...]
    early = jnp.where(odd, sibling, own)
    late = jnp.where(odd, own, sibling)
    rate = late[:, :LANES]
    fields = [early[:, :LANES] * rate]
    for q in range(1, FIELDS):
        part = slice(q * LANES, (q + 1) * LANES)
        fields.append(rate * early[:, part] + late[:, part])
    for target in range(out_ref.shape[0]):
        later = target > place_ref[1]
        for q, field in enumerate(fields):
            blank = 1.0 if q == 0 else 0.0
            out_ref[target, :, q * LANES : (q + 1) * LANES] = jnp.where(later, field, blank)


def sigma_kernel(
    place_ref, all_ref, own_ref, sibling_ref, picked_ref, h_ref, h2_ref, h4_ref, zeta_ref, hat_ref,
    forward_ref, inverse_ref, out_ref,
):
    state = [jnp.zeros((2, LANES), jnp.float32)] * TERMS

    def advance(rate, part, state):
        return [rate * m + part(q) for q, m in enumerate(state, 1)]

    for t in range(all_ref.shape[0]):
        state = advance(
            all_ref[t, :, :LANES], lambda q, t=t: all_ref[t, :, q * LANES : (q + 1) * LANES], state
        )
    odd = place_ref[2] == 1
    further = advance(
        sibling_ref[:, :LANES], lambda q: sibling_ref[:, q * LANES : (q + 1) * LANES], state
    )
    state = [jnp.where(odd, f, m) for f, m in zip(further, state)]
    z = zeta_ref[...]
    incoming = []
    for half in range(2):
        rows = [m[half : half + 1] for m in state]
        acc = jnp.broadcast_to(rows[7], (NE, LANES))
        for term in reversed(rows[:7]):
            acc = term + z * acc
        incoming.append(z * acc)
    incoming = jnp.concatenate(incoming, axis=1)
    incoming = jnp.concatenate([incoming, incoming], axis=0)
    zeta = jnp.concatenate([z, z], axis=1)
    zeta = jnp.concatenate([zeta, zeta], axis=0)
    picked = picked_ref[...]
    y = picked * incoming
    y = y + zeta * dot(y, h_ref[...])
    zeta2 = zeta * zeta
    y = y + zeta2 * dot(y, h2_ref[...])
    y = y + (zeta2 * zeta2) * dot(y, h4_ref[...])
    dressed = picked + zeta * y
    dressed = jnp.concatenate([dressed[:NE], dressed[NE:]], axis=1)
    green = dot(forward_ref[...], dressed)
    screen = hat_ref[...]
    half = NE // 2
    gc, gs, sc, ss = green[:half], green[half:], screen[:half], screen[half:]
    edge = lax.broadcasted_iota(jnp.int32, gc.shape, 0) == 0
    cc, s2 = gc * sc, gs * ss
    real = jnp.where(edge, cc, cc - s2)
    imag = jnp.where(edge, s2, gc * ss + gs * sc)
    out_ref[...] = dot(inverse_ref[...], jnp.concatenate([real, imag], axis=0))


def call(kernel, outs, n_scalars, n_arrays, flops=0, nbytes=0):
    shapes = [jax.ShapeDtypeStruct(s, jnp.float32) for s in outs]
    many = len(shapes) > 1
    vmem, smem = pl.BlockSpec(memory_space=pltpu.VMEM), pl.BlockSpec(memory_space=pltpu.SMEM)
    return pl.pallas_call(
        kernel,
        out_shape=shapes if many else shapes[0],
        in_specs=[smem] * n_scalars + [vmem] * n_arrays,
        out_specs=[vmem] * len(outs) if many else vmem,
        compiler_params=pltpu.CompilerParams(vmem_limit_bytes=VMEM_LIMIT),
        cost_estimate=pl.CostEstimate(flops=flops, bytes_accessed=nbytes, transcendentals=0),
    )


def powers(h, decay, coupling):
    shapes = [(2, FIELDS * LANES), (BS, BS), (BS, BS)]
    return call(powers_kernel, shapes, 0, 3, 6 * 8 * BS**3, 4 * 3 * BS * BS)(h, decay, coupling)


def pick(place, rows, h, h2, h4, zeta, screen, forward):
    shapes = [(2 * NE, BS), (NE, 2 * BS)]
    return call(picked_kernel, shapes, 2, 6, 6 * 2 * NE * NE * 2 * BS, 4 * 8 * BS * BS)(
        place, rows, h, h2, h4, zeta, screen, forward
    )


def compose(place, own, sibling, pairs):
    return call(compose_kernel, [(pairs, 2, FIELDS * LANES)], 1, 2, 0, 4 * pairs * 2 * FIELDS * LANES)(
        place, own, sibling
    )


def convolve(place, everyone, own, sibling, picked, h, h2, h4, zeta, hat, forward, inverse):
    return call(sigma_kernel, [(NE, 2 * BS)], 1, 11, 6 * 2 * 4 * BS**3, 4 * 8 * BS * BS)(
        place, everyone, own, sibling, picked, h, h2, h4, zeta, hat, forward, inverse
    )


def shards(hamiltonian, decay, coupling, rows, screened):
    pairs = lax.axis_size("pair")
    zeta, forward, inverse = (jnp.asarray(t) for t in tables())
    place = jnp.stack([lax.axis_index(name) for name in ("energy", "pair", "core")]).astype(jnp.int32)
    own, h2, h4 = powers(hamiltonian, decay, coupling)
    sibling = lax.ppermute(own, "core", [(0, 1), (1, 0)])
    picked, hat = pick(place, rows[0], hamiltonian, h2, h4, zeta, screened[0].reshape(NE, 2 * BS), forward)
    sent = compose(place, own, sibling, pairs)
    everyone = lax.all_to_all(sent, "pair", split_axis=0, concat_axis=0, tiled=True)
    sigma = convolve(place, everyone, own, sibling, picked, hamiltonian, h2, h4, zeta, hat, forward, inverse)
    return lax.all_to_all(sigma.reshape(NE, 2, BS), "energy", split_axis=0, concat_axis=1, tiled=True)


def solution(mesh):
    energies, slabs = mesh.devices.shape
    fine = Mesh(mesh.devices.reshape(energies, slabs // 2, 2), ("energy", "pair", "core"))
    slab = ("pair", "core")
    in_specs = (P(slab, None), P(slab, None), P(slab, None), P(slab, None), P(slab, None, "energy", None))
    out_specs = P("energy", slab, None)
    return jax.shard_map(shards, mesh=fine, in_specs=in_specs, out_specs=out_specs, check_vma=False)
```

```python
import math

import jax
import jax.numpy as jnp
import ml_dtypes
import numpy as np
from jax import lax
from jax.experimental import pallas as pl
from jax.experimental.pallas import tpu as pltpu
from jax.sharding import Mesh
from jax.sharding import PartitionSpec as P

BS = 256
NE = 128
SLABS = 64
LANES = 128
WIDE = 2 * BS
TERMS = 8
FIELDS = TERMS + 1
RECORD = FIELDS * LANES
VMEM_LIMIT = 48 * 1024 * 1024
WHOLE_VMEM = 60 * 1024 * 1024
HIGHEST = lax.Precision.HIGHEST


def tables():
    k = np.arange(NE)
    zeta = np.broadcast_to((1.0 / (1.0 + k / NE))[:, None], (NE, LANES))
    half = NE // 2
    angle = 2.0 * math.pi / NE * (np.arange(half)[:, None] * k[None, :] % NE)
    cosine, sine = np.cos(angle), np.sin(angle)
    sine[0] = (-1.0) ** k
    weight = np.full((half, 1), 2.0)
    weight[0] = 1.0
    forward = np.concatenate([cosine, sine], axis=0)
    inverse = np.concatenate([cosine * weight, sine * weight], axis=0).T / NE
    return tuple(np.ascontiguousarray(t, dtype=np.float32) for t in (zeta, forward, inverse))


def dot(a, b):
    return jnp.dot(a, b, precision=HIGHEST, preferred_element_type=jnp.float32)


def split(a):
    high = a.astype(jnp.bfloat16)
    return high, (a - high.astype(jnp.float32)).astype(jnp.bfloat16)


def left(a):
    high, low = split(a)
    return jnp.concatenate([high, low, high], axis=1)


def right(a):
    high, low = split(a)
    return jnp.concatenate([high, high, low], axis=0)


def product(a, b):
    return jnp.dot(a, b, preferred_element_type=jnp.float32)


def powers_kernel(h_hbm, decay_hbm, coupling_hbm, sent_ref, h_ref, decay_ref, coupling_ref, sems):
    copies = [
        pltpu.make_async_copy(source, target, sems.at[i])
        for i, (source, target) in enumerate(
            ((h_hbm, h_ref), (decay_hbm, decay_ref), (coupling_hbm, coupling_ref))
        )
    ]
    for copy in copies:
        copy.start()
    for copy in copies:
        copy.wait()
    h = h_ref[...]
    ht = h.T
    h2 = dot(h, h)
    h2t = dot(ht, ht)
    h4 = dot(h2, h2)
    h3t = dot(h2t, ht)
    row = lax.broadcasted_iota(jnp.int32, (BS, BS), 0)
    column = lax.broadcasted_iota(jnp.int32, (BS, BS), 1)
    share = coupling_ref[...] * (1.0 / SLABS)
    fields = [decay_ref[...], share]
    for diagonal in (
        jnp.where(row == column, h, 0.0),
        h * ht,
        h2 * ht,
        h2 * h2t,
        h4 * ht,
        h4 * h2t,
        h4 * h3t,
    ):
        fields.append(share * jnp.sum(diagonal, axis=0, keepdims=True))
    for q, field in enumerate(fields):
        both = jnp.concatenate([field[:, :LANES], field[:, LANES:]], axis=0)
        for target in range(sent_ref.shape[0]):
            sent_ref[target, :, q * LANES : (q + 1) * LANES] = both


def picked_kernel(
    place_ref, rows_ref, h_ref, zeta_ref, screen_ref, forward_ref,
    picked_ref, hat_ref, r1_ref, r2_ref, r4_ref, h2_ref, h4_ref,
):
    h2_ref[...] = dot(h_ref[...], h_ref[...])
    h4_ref[...] = dot(h2_ref[...], h2_ref[...])
    first = place_ref[0] * 2
    column = lax.broadcasted_iota(jnp.int32, (1, BS), 1)
    z = zeta_ref[...]
    zeta = jnp.concatenate([z, z], axis=1)
    v0, v1, v2, v4 = [], [], [], []
    for r in range(2):
        row = rows_ref[first + r]
        v0.append(jnp.where(column == row, 1.0, 0.0))
        v1.append(h_ref[pl.ds(row, 1), :])
        v2.append(h2_ref[pl.ds(row, 1), :])
        v4.append(h4_ref[pl.ds(row, 1), :])
    blank = jnp.zeros((6, BS), jnp.float32)
    v3 = dot(jnp.concatenate([*v1, blank], axis=0), h2_ref[...])
    late = dot(jnp.concatenate([*v1, *v2, v3[:2], blank[:2]], axis=0), h4_ref[...])
    for r in range(2):
        series = [v0[r], v1[r], v2[r], v3[r : r + 1], v4[r]]
        series += [late[2 * j + r : 2 * j + r + 1] for j in range(3)]
        acc = jnp.broadcast_to(series[7], (NE, BS))
        for term in reversed(series[:7]):
            acc = term + zeta * acc
        picked_ref[r * NE : (r + 1) * NE, :] = zeta * acc
    hat_ref[...] = dot(forward_ref[...], screen_ref[...])
    r1_ref[...] = right(h_ref[...])
    r2_ref[...] = right(h2_ref[...])
    r4_ref[...] = right(h4_ref[...])


def follow(record, state):
    rate, parts = record[0], record[1:]
    if len(state) == FIELDS:
        return [rate * state[0]] + [rate * m + part for m, part in zip(state[1:], parts)]
    return [rate * m + part for m, part in zip(state, parts)]


def fields_of(ref, i):
    return [ref[i, :, q * LANES : (q + 1) * LANES] for q in range(FIELDS)]


def compose_kernel(place_ref, row_ref, sent_ref, before_ref):
    mine = place_ref[2]
    blank = [jnp.ones((2, LANES), jnp.float32)] + [jnp.zeros((2, LANES), jnp.float32)] * TERMS
    state, before = blank, blank
    for t in range(row_ref.shape[0]):
        before = [jnp.where(mine == t, new, old) for new, old in zip(state, before)]
        state = follow(fields_of(row_ref, t), state)
    for q in range(FIELDS):
        part = slice(q * LANES, (q + 1) * LANES)
        before_ref[:, part] = before[q]
        for target in range(sent_ref.shape[0]):
            sent_ref[target, :, part] = jnp.where(target > place_ref[1], state[q], blank[q])


def sigma_kernel(
    place_ref, lines_ref, before_ref, picked_ref, r1_ref, r2_ref, r4_ref, zeta_ref, hat_ref,
    forward_ref, inverse_ref, out_ref,
):
    state = [jnp.zeros((2, LANES), jnp.float32)] * TERMS
    for t in range(lines_ref.shape[0]):
        state = follow(fields_of(lines_ref, t), state)
    state = follow([before_ref[:, q * LANES : (q + 1) * LANES] for q in range(FIELDS)], state)
    z = zeta_ref[...]
    incoming = []
    for half in range(2):
        rows = [m[half : half + 1] for m in state]
        acc = jnp.broadcast_to(rows[7], (NE, LANES))
        for term in reversed(rows[:7]):
            acc = term + z * acc
        incoming.append(z * acc)
    incoming = jnp.concatenate(incoming, axis=1)
    incoming = jnp.concatenate([incoming, incoming], axis=0)
    zeta = jnp.concatenate([z, z], axis=1)
    zeta = jnp.concatenate([zeta, zeta], axis=0)
    picked = picked_ref[...]
    y = picked * incoming
    y = y + zeta * product(left(y), r1_ref[...])
    zeta2 = zeta * zeta
    y = y + zeta2 * product(left(y), r2_ref[...])
    y = y + (zeta2 * zeta2) * product(left(y), r4_ref[...])
    dressed = picked + zeta * y
    dressed = jnp.concatenate([dressed[:NE], dressed[NE:]], axis=1)
    green = product(forward_ref[...], right(dressed))
    screen = hat_ref[...]
    half = NE // 2
    gc, gs, sc, ss = green[:half], green[half:], screen[:half], screen[half:]
    edge = lax.broadcasted_iota(jnp.int32, gc.shape, 0) == 0
    cc, s2 = gc * sc, gs * ss
    real = jnp.where(edge, cc, cc - s2)
    imag = jnp.where(edge, s2, gc * ss + gs * sc)
    out_ref[...] = product(inverse_ref[...], right(jnp.concatenate([real, imag], axis=0)))


def call(kernel, outs, in_spaces, scratch=(), flops=0, nbytes=0, limit=VMEM_LIMIT):
    shapes = [jax.ShapeDtypeStruct(s, d) for s, d in outs]
    spaces = {"v": pltpu.VMEM, "s": pltpu.SMEM, "h": pltpu.HBM}
    return pl.pallas_call(
        kernel,
        out_shape=shapes,
        in_specs=[pl.BlockSpec(memory_space=spaces[c]) for c in in_spaces],
        out_specs=[pl.BlockSpec(memory_space=pltpu.VMEM)] * len(outs),
        scratch_shapes=scratch,
        compiler_params=pltpu.CompilerParams(vmem_limit_bytes=limit),
        cost_estimate=pl.CostEstimate(flops=flops, bytes_accessed=nbytes, transcendentals=0),
    )


def powers(h, decay, coupling, copies):
    f32 = jnp.float32
    outs = [((copies, 2, RECORD), f32)]
    scratch = [pltpu.VMEM(s, f32) for s in ((BS, BS), (1, BS), (1, BS))] + [pltpu.SemaphoreType.DMA((3,))]
    return call(powers_kernel, outs, "hhh", scratch, 48 * BS**3, 4 * 2 * BS * BS, WHOLE_VMEM)(
        h, decay, coupling
    )[0]


def pick(place, rows, h, zeta, screen, forward):
    outs = [((2 * NE, BS), jnp.float32), ((NE, WIDE), jnp.float32)] + [((3 * BS, BS), jnp.bfloat16)] * 3
    scratch = [pltpu.VMEM((BS, BS), jnp.float32)] * 2
    return call(picked_kernel, outs, "ssvvvv", scratch, 36 * BS**3, 4 * 12 * BS * BS)(
        place, rows, h, zeta, screen, forward
    )


def compose(place, row, copies):
    outs = [((copies, 2, RECORD), jnp.float32), ((2, RECORD), jnp.float32)]
    return call(compose_kernel, outs, "sv", (), 0, 4 * 2 * copies * 2 * RECORD)(place, row)


def convolve(place, lines, before, picked, rights, zeta, hat, forward, inverse):
    outs = [((NE, WIDE), jnp.float32)]
    return call(sigma_kernel, outs, "svvvvvvvvvv", (), 6 * 4 * BS**3, 4 * 8 * BS * BS)(
        place, lines, before, picked, *rights, zeta, hat, forward, inverse
    )[0]


def constants():
    zeta, forward, inverse = tables()
    def wide(t):
        high = t.astype(ml_dtypes.bfloat16)
        low = (t - high.astype(np.float32)).astype(ml_dtypes.bfloat16)
        return jnp.asarray(np.concatenate([high, low, high], axis=1))
    return jnp.asarray(zeta), jnp.asarray(forward), wide(forward), wide(inverse)


def shards(hamiltonian, decay, coupling, rows, screened):
    zeta, forward, forward3, inverse3 = constants()
    place = jnp.stack([lax.axis_index(name) for name in ("energy", "line", "member")]).astype(jnp.int32)
    sent = powers(hamiltonian, decay, coupling, lax.axis_size("member"))
    row = lax.all_to_all(sent, "member", split_axis=0, concat_axis=0, tiled=True)
    screen = screened[0].reshape(NE, WIDE)
    picked, hat, *rights = pick(place, rows[0], hamiltonian, zeta, screen, forward)
    sent, before = compose(place, row, lax.axis_size("line"))
    lines = lax.all_to_all(sent, "line", split_axis=0, concat_axis=0, tiled=True)
    sigma = convolve(place, lines, before, picked, rights, zeta, hat, forward3, inverse3)
    return lax.all_to_all(sigma.reshape(NE, 2, BS), "energy", split_axis=0, concat_axis=1, tiled=True)


def solution(mesh):
    energies, slabs = mesh.devices.shape
    fine = Mesh(mesh.devices.reshape(energies, slabs // 8, 8), ("energy", "line", "member"))
    slab = ("line", "member")
    in_specs = (P(slab, None), P(slab, None), P(slab, None), P(slab, None), P(slab, None, "energy", None))
    out_specs = P("energy", slab, None)
    return jax.shard_map(shards, mesh=fine, in_specs=in_specs, out_specs=out_specs, check_vma=False)
```

```python
import math

import jax
import jax.numpy as jnp
import ml_dtypes
import numpy as np
from jax import lax
from jax.experimental import pallas as pl
from jax.experimental.pallas import tpu as pltpu
from jax.sharding import Mesh
from jax.sharding import PartitionSpec as P

BS = 256
NE = 128
SLABS = 64
LANES = 128
WIDE = 2 * BS
TERMS = 8
FIELDS = TERMS + 1
RECORD = FIELDS * LANES
VMEM_LIMIT = 48 * 1024 * 1024
HIGHEST = lax.Precision.HIGHEST


def tables():
    k = np.arange(NE)
    zeta = np.broadcast_to((1.0 / (1.0 + k / NE))[:, None], (NE, LANES))
    half = NE // 2
    angle = 2.0 * math.pi / NE * (np.arange(half)[:, None] * k[None, :] % NE)
    cosine, sine = np.cos(angle), np.sin(angle)
    sine[0] = (-1.0) ** k
    weight = np.full((half, 1), 2.0)
    weight[0] = 1.0
    forward = np.concatenate([cosine, sine], axis=0)
    inverse = np.concatenate([cosine * weight, sine * weight], axis=0).T / NE
    return tuple(np.ascontiguousarray(t, dtype=np.float32) for t in (zeta, forward, inverse))


def dot(a, b):
    return jnp.dot(a, b, precision=HIGHEST, preferred_element_type=jnp.float32)


def split(a):
    high = a.astype(jnp.bfloat16)
    return high, (a - high.astype(jnp.float32)).astype(jnp.bfloat16)


def left(a):
    high, low = split(a)
    return jnp.concatenate([high, low, high], axis=1)


def right(a):
    high, low = split(a)
    return jnp.concatenate([high, high, low], axis=0)


def product(a, b):
    return jnp.dot(a, b, preferred_element_type=jnp.float32)


def powers_kernel(h_hbm, decay_hbm, coupling_hbm, sent_ref, h_ref, decay_ref, coupling_ref, sems):
    copies = [
        pltpu.make_async_copy(source, target, sems.at[i])
        for i, (source, target) in enumerate(
            ((h_hbm, h_ref), (decay_hbm, decay_ref), (coupling_hbm, coupling_ref))
        )
    ]
    for copy in copies:
        copy.start()
    for copy in copies:
        copy.wait()
    h = h_ref[...]
    ht = h.T
    right_ht = right(ht)
    h2 = product(left(h), right(h))
    h2t = product(left(ht), right_ht)
    h4 = product(left(h2), right(h2))
    h3t = product(left(h2t), right_ht)
    row = lax.broadcasted_iota(jnp.int32, (BS, BS), 0)
    column = lax.broadcasted_iota(jnp.int32, (BS, BS), 1)
    share = coupling_ref[...] * (1.0 / SLABS)
    fields = [decay_ref[...], share]
    for diagonal in (
        jnp.where(row == column, h, 0.0),
        h * ht,
        h2 * ht,
        h2 * h2t,
        h4 * ht,
        h4 * h2t,
        h4 * h3t,
    ):
        fields.append(share * jnp.sum(diagonal, axis=0, keepdims=True))
    for q, field in enumerate(fields):
        both = jnp.concatenate([field[:, :LANES], field[:, LANES:]], axis=0)
        for target in range(sent_ref.shape[0]):
            sent_ref[target, :, q * LANES : (q + 1) * LANES] = both


def picked_kernel(
    rows_ref, h_ref, zeta_ref, screen_ref, forward_ref, picked_ref, hat_ref, r1_ref, r2_ref, r4_ref, h2_ref, h4_ref
):
    r1_ref[...] = right(h_ref[...])
    h2_ref[...] = product(left(h_ref[...]), r1_ref[...])
    r2_ref[...] = right(h2_ref[...])
    h4_ref[...] = product(left(h2_ref[...]), r2_ref[...])
    r4_ref[...] = right(h4_ref[...])
    column = lax.broadcasted_iota(jnp.int32, (1, BS), 1)
    z = zeta_ref[...]
    zeta = jnp.concatenate([z, z], axis=1)
    v0, v1, v2, v4 = [], [], [], []
    for r in range(2):
        row = rows_ref[r]
        v0.append(jnp.where(column == row, 1.0, 0.0))
        v1.append(h_ref[pl.ds(row, 1), :])
        v2.append(h2_ref[pl.ds(row, 1), :])
        v4.append(h4_ref[pl.ds(row, 1), :])
    blank = jnp.zeros((6, BS), jnp.float32)
    v3 = product(left(jnp.concatenate([*v1, blank], axis=0)), r2_ref[...])
    late = product(left(jnp.concatenate([*v1, *v2, v3[:2], blank[:2]], axis=0)), r4_ref[...])
    for r in range(2):
        series = [v0[r], v1[r], v2[r], v3[r : r + 1], v4[r]]
        series += [late[2 * j + r : 2 * j + r + 1] for j in range(3)]
        acc = jnp.broadcast_to(series[7], (NE, BS))
        for term in reversed(series[:7]):
            acc = term + zeta * acc
        picked_ref[r * NE : (r + 1) * NE, :] = zeta * acc
    hat_ref[...] = product(forward_ref[...], right(screen_ref[...]))


def follow(record, state):
    rate, parts = record[0], record[1:]
    if len(state) == FIELDS:
        return [rate * state[0]] + [rate * m + part for m, part in zip(state[1:], parts)]
    return [rate * m + part for m, part in zip(state, parts)]


def fields_of(ref, i):
    return [ref[i, :, q * LANES : (q + 1) * LANES] for q in range(FIELDS)]


def compose_kernel(place_ref, row_ref, sent_ref, before_ref):
    line, mine = place_ref[0:1, :], place_ref[1:2, :]
    blank = [jnp.ones((2, LANES), jnp.float32)] + [jnp.zeros((2, LANES), jnp.float32)] * TERMS
    state, before = blank, blank
    for t in range(row_ref.shape[0]):
        before = [jnp.where(mine == t, new, old) for new, old in zip(state, before)]
        state = follow(fields_of(row_ref, t), state)
    for q in range(FIELDS):
        part = slice(q * LANES, (q + 1) * LANES)
        before_ref[:, part] = before[q]
        for target in range(sent_ref.shape[0]):
            sent_ref[target, :, part] = jnp.where(line < target, state[q], blank[q])


def sigma_kernel(
    lines_ref, before_ref, picked_ref, r1_ref, r2_ref, r4_ref, zeta_ref, hat_ref,
    forward_ref, inverse_ref, out_ref,
):
    state = [jnp.zeros((2, LANES), jnp.float32)] * TERMS
    for t in range(lines_ref.shape[0]):
        state = follow(fields_of(lines_ref, t), state)
    state = follow([before_ref[:, q * LANES : (q + 1) * LANES] for q in range(FIELDS)], state)
    z = zeta_ref[...]
    incoming = []
    for half in range(2):
        rows = [m[half : half + 1] for m in state]
        acc = jnp.broadcast_to(rows[7], (NE, LANES))
        for term in reversed(rows[:7]):
            acc = term + z * acc
        incoming.append(z * acc)
    incoming = jnp.concatenate(incoming, axis=1)
    incoming = jnp.concatenate([incoming, incoming], axis=0)
    zeta = jnp.concatenate([z, z], axis=1)
    zeta = jnp.concatenate([zeta, zeta], axis=0)
    picked = picked_ref[...]
    y = picked * incoming
    y = y + zeta * product(left(y), r1_ref[...])
    zeta2 = zeta * zeta
    y = y + zeta2 * product(left(y), r2_ref[...])
    y = y + (zeta2 * zeta2) * product(left(y), r4_ref[...])
    dressed = picked + zeta * y
    dressed = jnp.concatenate([dressed[:NE], dressed[NE:]], axis=1)
    green = product(forward_ref[...], right(dressed))
    screen = hat_ref[...]
    half = NE // 2
    gc, gs, sc, ss = green[:half], green[half:], screen[:half], screen[half:]
    edge = lax.broadcasted_iota(jnp.int32, gc.shape, 0) == 0
    cc, s2 = gc * sc, gs * ss
    real = jnp.where(edge, cc, cc - s2)
    imag = jnp.where(edge, s2, gc * ss + gs * sc)
    out_ref[...] = product(inverse_ref[...], right(jnp.concatenate([real, imag], axis=0)))


def call(kernel, outs, in_spaces, scratch=(), flops=0, nbytes=0):
    shapes = [jax.ShapeDtypeStruct(s, d) for s, d in outs]
    spaces = {"v": pltpu.VMEM, "s": pltpu.SMEM, "h": pltpu.HBM}
    return pl.pallas_call(
        kernel,
        out_shape=shapes,
        in_specs=[pl.BlockSpec(memory_space=spaces[c]) for c in in_spaces],
        out_specs=[pl.BlockSpec(memory_space=pltpu.VMEM)] * len(outs),
        scratch_shapes=scratch,
        compiler_params=pltpu.CompilerParams(vmem_limit_bytes=VMEM_LIMIT),
        cost_estimate=pl.CostEstimate(flops=flops, bytes_accessed=nbytes, transcendentals=0),
    )


def powers(h, decay, coupling, copies):
    f32 = jnp.float32
    outs = [((copies, 2, RECORD), f32)]
    h, decay, coupling = (pltpu.with_memory_space_constraint(a, pltpu.HBM) for a in (h, decay, coupling))
    scratch = [pltpu.VMEM(s, f32) for s in ((BS, BS), (1, BS), (1, BS))] + [pltpu.SemaphoreType.DMA((3,))]
    return call(powers_kernel, outs, "hhh", scratch, 48 * BS**3, 4 * 2 * BS * BS)(
        h, decay, coupling
    )[0]


def pick(rows, h, zeta, screen, forward):
    outs = [((2 * NE, BS), jnp.float32), ((NE, WIDE), jnp.float32)] + [((3 * BS, BS), jnp.bfloat16)] * 3
    scratch = [pltpu.VMEM((BS, BS), jnp.float32)] * 2
    return call(picked_kernel, outs, "svvvv", scratch, 24 * BS**3, 4 * 12 * BS * BS)(
        rows, h, zeta, screen, forward
    )


def compose(place, row, copies):
    outs = [((copies, 2, RECORD), jnp.float32), ((2, RECORD), jnp.float32)]
    return call(compose_kernel, outs, "vv", (), 0, 4 * 2 * copies * 2 * RECORD)(place, row)


def convolve(lines, before, picked, rights, zeta, hat, forward, inverse):
    outs = [((NE, WIDE), jnp.float32)]
    return call(sigma_kernel, outs, "vvvvvvvvvv", (), 6 * 4 * BS**3, 4 * 8 * BS * BS)(
        lines, before, picked, *rights, zeta, hat, forward, inverse
    )[0]


def constants():
    zeta, forward, inverse = tables()
    def wide(t):
        high = t.astype(ml_dtypes.bfloat16)
        low = (t - high.astype(np.float32)).astype(ml_dtypes.bfloat16)
        return jnp.asarray(np.concatenate([high, low, high], axis=1))
    return jnp.asarray(zeta), wide(forward), wide(inverse)


def shards(hamiltonian, decay, coupling, rows, screened):
    zeta, forward, inverse = constants()
    place = jnp.stack([jnp.full((LANES,), lax.axis_index(name), jnp.int32) for name in ("line", "member")])
    sent = powers(hamiltonian, decay, coupling, lax.axis_size("member"))
    sent, place = lax.optimization_barrier((sent, place))
    row = lax.all_to_all(sent, "member", split_axis=0, concat_axis=0, tiled=True)
    row, rows = lax.optimization_barrier((row, rows))
    mine = lax.dynamic_slice(rows[0], (2 * lax.axis_index("energy"),), (2,))
    picked, hat, *rights = pick(mine, hamiltonian, zeta, screened[0].reshape(NE, WIDE), forward)
    sent, before = compose(place, row, lax.axis_size("line"))
    lines = lax.all_to_all(sent, "line", split_axis=0, concat_axis=0, tiled=True)
    sigma = convolve(lines, before, picked, rights, zeta, hat, forward, inverse)
    return lax.all_to_all(sigma.reshape(NE, 2, BS), "energy", split_axis=0, concat_axis=1, tiled=True)


def solution(mesh):
    energies, slabs = mesh.devices.shape
    fine = Mesh(mesh.devices.reshape(energies, slabs // 8, 8), ("energy", "line", "member"))
    slab = ("line", "member")
    in_specs = (P(slab, None), P(slab, None), P(slab, None), P(slab, None), P(slab, None, "energy", None))
    out_specs = P("energy", slab, None)
    return jax.shard_map(shards, mesh=fine, in_specs=in_specs, out_specs=out_specs, check_vma=False)
```

```python
import math

import jax
import jax.numpy as jnp
import ml_dtypes
import numpy as np
from jax import lax
from jax.experimental import pallas as pl
from jax.experimental.pallas import tpu as pltpu
from jax.sharding import Mesh
from jax.sharding import PartitionSpec as P

BS = 256
NE = 128
SLABS = 64
LANES = 128
WIDE = 2 * BS
TERMS = 8
FIELDS = TERMS + 1
RECORD = FIELDS * LANES
VMEM_LIMIT = 48 * 1024 * 1024
HIGHEST = lax.Precision.HIGHEST


def tables():
    k = np.arange(NE)
    zeta = np.broadcast_to((1.0 / (1.0 + k / NE))[:, None], (NE, LANES))
    half = NE // 2
    angle = 2.0 * math.pi / NE * (np.arange(half)[:, None] * k[None, :] % NE)
    cosine, sine = np.cos(angle), np.sin(angle)
    sine[0] = (-1.0) ** k
    weight = np.full((half, 1), 2.0)
    weight[0] = 1.0
    forward = np.concatenate([cosine, sine], axis=0)
    inverse = np.concatenate([cosine * weight, sine * weight], axis=0).T / NE
    return tuple(np.ascontiguousarray(t, dtype=np.float32) for t in (zeta, forward, inverse))


def dot(a, b):
    return jnp.dot(a, b, precision=HIGHEST, preferred_element_type=jnp.float32)


def split(a):
    high = a.astype(jnp.bfloat16)
    return high, (a - high.astype(jnp.float32)).astype(jnp.bfloat16)


def left(a):
    high, low = split(a)
    return jnp.concatenate([high, low, high], axis=1)


def right(a):
    high, low = split(a)
    return jnp.concatenate([high, high, low], axis=0)


def product(a, b):
    return jnp.dot(a, b, preferred_element_type=jnp.float32)


def powers_kernel(h_hbm, decay_hbm, coupling_hbm, sent_ref, h_ref, decay_ref, coupling_ref, sems):
    copies = [
        pltpu.make_async_copy(source, target, sems.at[i])
        for i, (source, target) in enumerate(
            ((h_hbm, h_ref), (decay_hbm, decay_ref), (coupling_hbm, coupling_ref))
        )
    ]
    for copy in copies:
        copy.start()
    for copy in copies:
        copy.wait()
    h = h_ref[...]
    ht = h.T
    right_ht = right(ht)
    h2 = product(left(h), right(h))
    h2t = product(left(ht), right_ht)
    h4 = product(left(h2), right(h2))
    h3t = product(left(h2t), right_ht)
    row = lax.broadcasted_iota(jnp.int32, (BS, BS), 0)
    column = lax.broadcasted_iota(jnp.int32, (BS, BS), 1)
    share = coupling_ref[...] * (1.0 / SLABS)
    fields = [decay_ref[...], share]
    for diagonal in (
        jnp.where(row == column, h, 0.0),
        h * ht,
        h2 * ht,
        h2 * h2t,
        h4 * ht,
        h4 * h2t,
        h4 * h3t,
    ):
        fields.append(share * jnp.sum(diagonal, axis=0, keepdims=True))
    for q, field in enumerate(fields):
        both = jnp.concatenate([field[:, :LANES], field[:, LANES:]], axis=0)
        for target in range(sent_ref.shape[0]):
            sent_ref[target, :, q * LANES : (q + 1) * LANES] = both


def picked_kernel(
    rows_ref, h_ref, zeta_ref, screen_ref, forward_ref, picked_ref, hat_ref, r1_ref, r2_ref, r4_ref, h2_ref, h4_ref
):
    r1_ref[...] = right(h_ref[...])
    h2_ref[...] = product(left(h_ref[...]), r1_ref[...])
    r2_ref[...] = right(h2_ref[...])
    h4_ref[...] = product(left(h2_ref[...]), r2_ref[...])
    r4_ref[...] = right(h4_ref[...])
    column = lax.broadcasted_iota(jnp.int32, (1, BS), 1)
    z = zeta_ref[...]
    zeta = jnp.concatenate([z, z], axis=1)
    v0, v1, v2, v4 = [], [], [], []
    for r in range(2):
        row = rows_ref[r]
        v0.append(jnp.where(column == row, 1.0, 0.0))
        v1.append(h_ref[pl.ds(row, 1), :])
        v2.append(h2_ref[pl.ds(row, 1), :])
        v4.append(h4_ref[pl.ds(row, 1), :])
    blank = jnp.zeros((6, BS), jnp.float32)
    v3 = product(left(jnp.concatenate([*v1, blank], axis=0)), r2_ref[...])
    late = product(left(jnp.concatenate([*v1, *v2, v3[:2], blank[:2]], axis=0)), r4_ref[...])
    for r in range(2):
        series = [v0[r], v1[r], v2[r], v3[r : r + 1], v4[r]]
        series += [late[2 * j + r : 2 * j + r + 1] for j in range(3)]
        acc = jnp.broadcast_to(series[7], (NE, BS))
        for term in reversed(series[:7]):
            acc = term + zeta * acc
        picked_ref[r * NE : (r + 1) * NE, :] = zeta * acc
    hat_ref[...] = product(forward_ref[...], right(screen_ref[...]))


def follow(record, state):
    rate, parts = record[0], record[1:]
    if len(state) == FIELDS:
        return [rate * state[0]] + [rate * m + part for m, part in zip(state[1:], parts)]
    return [rate * m + part for m, part in zip(state, parts)]


def fields_of(ref, i):
    return [ref[i, :, q * LANES : (q + 1) * LANES] for q in range(FIELDS)]


def compose_kernel(place_ref, row_ref, sent_ref, before_ref):
    line, mine = place_ref[0:1, :], place_ref[1:2, :]
    blank = [jnp.ones((2, LANES), jnp.float32)] + [jnp.zeros((2, LANES), jnp.float32)] * TERMS
    state, before = blank, blank
    for t in range(row_ref.shape[0]):
        before = [jnp.where(mine == t, new, old) for new, old in zip(state, before)]
        state = follow(fields_of(row_ref, t), state)
    for q in range(FIELDS):
        part = slice(q * LANES, (q + 1) * LANES)
        before_ref[:, part] = before[q]
        for target in range(sent_ref.shape[0]):
            sent_ref[target, :, part] = jnp.where(line < target, state[q], blank[q])


def sigma_kernel(
    lines_ref, before_ref, picked_ref, r1_ref, r2_ref, r4_ref, zeta_ref, hat_ref,
    forward_ref, inverse_ref, out_ref,
):
    state = [jnp.zeros((2, LANES), jnp.float32)] * TERMS
    for t in range(lines_ref.shape[0]):
        state = follow(fields_of(lines_ref, t), state)
    state = follow([before_ref[:, q * LANES : (q + 1) * LANES] for q in range(FIELDS)], state)
    z = zeta_ref[...]
    incoming = []
    for half in range(2):
        rows = [m[half : half + 1] for m in state]
        acc = jnp.broadcast_to(rows[7], (NE, LANES))
        for term in reversed(rows[:7]):
            acc = term + z * acc
        incoming.append(z * acc)
    incoming = jnp.concatenate(incoming, axis=1)
    incoming = jnp.concatenate([incoming, incoming], axis=0)
    zeta = jnp.concatenate([z, z], axis=1)
    zeta = jnp.concatenate([zeta, zeta], axis=0)
    picked = picked_ref[...]
    y = picked * incoming
    y = y + zeta * product(left(y), r1_ref[...])
    zeta2 = zeta * zeta
    y = y + zeta2 * product(left(y), r2_ref[...])
    y = y + (zeta2 * zeta2) * product(left(y), r4_ref[...])
    dressed = picked + zeta * y
    dressed = jnp.concatenate([dressed[:NE], dressed[NE:]], axis=1)
    green = product(forward_ref[...], right(dressed))
    screen = hat_ref[...]
    half = NE // 2
    gc, gs, sc, ss = green[:half], green[half:], screen[:half], screen[half:]
    edge = lax.broadcasted_iota(jnp.int32, gc.shape, 0) == 0
    cc, s2 = gc * sc, gs * ss
    real = jnp.where(edge, cc, cc - s2)
    imag = jnp.where(edge, s2, gc * ss + gs * sc)
    out_ref[...] = product(inverse_ref[...], right(jnp.concatenate([real, imag], axis=0)))


def call(kernel, outs, in_spaces, scratch=(), flops=0, nbytes=0):
    shapes = [jax.ShapeDtypeStruct(s, d) for s, d in outs]
    spaces = {"v": pltpu.VMEM, "s": pltpu.SMEM, "h": pltpu.HBM}
    return pl.pallas_call(
        kernel,
        out_shape=shapes,
        in_specs=[pl.BlockSpec(memory_space=spaces[c]) for c in in_spaces],
        out_specs=[pl.BlockSpec(memory_space=pltpu.VMEM)] * len(outs),
        scratch_shapes=scratch,
        compiler_params=pltpu.CompilerParams(vmem_limit_bytes=VMEM_LIMIT),
        cost_estimate=pl.CostEstimate(flops=flops, bytes_accessed=nbytes, transcendentals=0),
    )


def powers(h, decay, coupling, copies):
    f32 = jnp.float32
    outs = [((copies, 2, RECORD), f32)]
    h, decay, coupling = (pltpu.with_memory_space_constraint(a, pltpu.HBM) for a in (h, decay, coupling))
    scratch = [pltpu.VMEM(s, f32) for s in ((BS, BS), (1, BS), (1, BS))] + [pltpu.SemaphoreType.DMA((3,))]
    return call(powers_kernel, outs, "hhh", scratch, 48 * BS**3, 4 * 2 * BS * BS)(
        h, decay, coupling
    )[0]


def pick(rows, h, zeta, screen, forward):
    outs = [((2 * NE, BS), jnp.float32), ((NE, WIDE), jnp.float32)] + [((3 * BS, BS), jnp.bfloat16)] * 3
    scratch = [pltpu.VMEM((BS, BS), jnp.float32)] * 2
    return call(picked_kernel, outs, "svvvv", scratch, 24 * BS**3, 4 * 12 * BS * BS)(
        rows, h, zeta, screen, forward
    )


def compose(place, row, copies):
    outs = [((copies, 2, RECORD), jnp.float32), ((2, RECORD), jnp.float32)]
    return call(compose_kernel, outs, "vv", (), 0, 4 * 2 * copies * 2 * RECORD)(place, row)


def convolve(lines, before, picked, rights, zeta, hat, forward, inverse):
    outs = [((NE, WIDE), jnp.float32)]
    return call(sigma_kernel, outs, "vvvvvvvvvv", (), 6 * 4 * BS**3, 4 * 8 * BS * BS)(
        lines, before, picked, *rights, zeta, hat, forward, inverse
    )[0]


def constants():
    zeta, forward, inverse = tables()
    def wide(t):
        high = t.astype(ml_dtypes.bfloat16)
        low = (t - high.astype(np.float32)).astype(ml_dtypes.bfloat16)
        return jnp.asarray(np.concatenate([high, low, high], axis=1))
    return jnp.asarray(zeta), wide(forward), wide(inverse)


def shards(hamiltonian, decay, coupling, rows, screened):
    zeta, forward, inverse = constants()
    place = jnp.stack([jnp.full((LANES,), lax.axis_index(name), jnp.int32) for name in ("line", "member")])
    sent = powers(hamiltonian, decay, coupling, lax.axis_size("member"))
    own = 2 * lax.axis_index("energy")
    sent, place, own = lax.optimization_barrier((sent, place, own))
    row = lax.all_to_all(sent, "member", split_axis=0, concat_axis=0, tiled=True)
    row, rows, screened, own = lax.optimization_barrier((row, rows, screened, own))
    mine = lax.dynamic_slice(rows[0], (own,), (2,))
    picked, hat, *rights = pick(mine, hamiltonian, zeta, screened[0].reshape(NE, WIDE), forward)
    sent, before = compose(place, row, lax.axis_size("line"))
    lines = lax.all_to_all(sent, "line", split_axis=0, concat_axis=0, tiled=True)
    sigma = convolve(lines, before, picked, rights, zeta, hat, forward, inverse)
    return lax.all_to_all(sigma.reshape(NE, 2, BS), "energy", split_axis=0, concat_axis=1, tiled=True)


def solution(mesh):
    energies, slabs = mesh.devices.shape
    fine = Mesh(mesh.devices.reshape(energies, slabs // 8, 8), ("energy", "line", "member"))
    slab = ("line", "member")
    in_specs = (P(slab, None), P(slab, None), P(slab, None), P(slab, None), P(slab, None, "energy", None))
    out_specs = P("energy", slab, None)
    return jax.shard_map(shards, mesh=fine, in_specs=in_specs, out_specs=out_specs, check_vma=False)
```

```python
import math

import jax
import jax.numpy as jnp
import ml_dtypes
import numpy as np
from jax import lax
from jax.experimental import pallas as pl
from jax.experimental.pallas import tpu as pltpu
from jax.sharding import Mesh
from jax.sharding import PartitionSpec as P

BS = 256
NE = 128
SLABS = 64
LANES = 128
WIDE = 2 * BS
TERMS = 8
FIELDS = TERMS + 1
RECORD = FIELDS * LANES
VMEM_LIMIT = 48 * 1024 * 1024
HIGHEST = lax.Precision.HIGHEST


def tables():
    k = np.arange(NE)
    zeta = np.broadcast_to((1.0 / (1.0 + k / NE))[:, None], (NE, LANES))
    half = NE // 2
    angle = 2.0 * math.pi / NE * (np.arange(half)[:, None] * k[None, :] % NE)
    cosine, sine = np.cos(angle), np.sin(angle)
    sine[0] = (-1.0) ** k
    weight = np.full((half, 1), 2.0)
    weight[0] = 1.0
    forward = np.concatenate([cosine, sine], axis=0)
    inverse = np.concatenate([cosine * weight, sine * weight], axis=0).T / NE
    return tuple(np.ascontiguousarray(t, dtype=np.float32) for t in (zeta, forward, inverse))


def dot(a, b):
    return jnp.dot(a, b, precision=HIGHEST, preferred_element_type=jnp.float32)


def split(a):
    high = a.astype(jnp.bfloat16)
    return high, (a - high.astype(jnp.float32)).astype(jnp.bfloat16)


def left(a):
    high, low = split(a)
    return jnp.concatenate([high, low, high], axis=1)


def right(a):
    high, low = split(a)
    return jnp.concatenate([high, high, low], axis=0)


def product(a, b):
    return jnp.dot(a, b, preferred_element_type=jnp.float32)


def powers_kernel(h_hbm, decay_hbm, coupling_hbm, sent_ref, h_ref, decay_ref, coupling_ref, sems):
    copies = [
        pltpu.make_async_copy(source, target, sems.at[i])
        for i, (source, target) in enumerate(
            ((h_hbm, h_ref), (decay_hbm, decay_ref), (coupling_hbm, coupling_ref))
        )
    ]
    for copy in copies:
        copy.start()
    for copy in copies:
        copy.wait()
    h = h_ref[...]
    ht = h.T
    right_ht = right(ht)
    h2 = product(left(h), right(h))
    h2t = product(left(ht), right_ht)
    h4 = product(left(h2), right(h2))
    h3t = product(left(h2t), right_ht)
    row = lax.broadcasted_iota(jnp.int32, (BS, BS), 0)
    column = lax.broadcasted_iota(jnp.int32, (BS, BS), 1)
    share = coupling_ref[...] * (1.0 / SLABS)
    fields = [decay_ref[...], share]
    for diagonal in (
        jnp.where(row == column, h, 0.0),
        h * ht,
        h2 * ht,
        h2 * h2t,
        h4 * ht,
        h4 * h2t,
        h4 * h3t,
    ):
        fields.append(share * jnp.sum(diagonal, axis=0, keepdims=True))
    for q, field in enumerate(fields):
        both = jnp.concatenate([field[:, :LANES], field[:, LANES:]], axis=0)
        for target in range(sent_ref.shape[0]):
            sent_ref[target, :, q * LANES : (q + 1) * LANES] = both


def picked_kernel(
    rows_ref, h_ref, zeta_ref, screen_ref, forward_ref, picked_ref, hat_ref, r1_ref, r2_ref, r4_ref, h2_ref, h4_ref
):
    r1_ref[...] = right(h_ref[...])
    h2_ref[...] = product(left(h_ref[...]), r1_ref[...])
    r2_ref[...] = right(h2_ref[...])
    h4_ref[...] = product(left(h2_ref[...]), r2_ref[...])
    r4_ref[...] = right(h4_ref[...])
    column = lax.broadcasted_iota(jnp.int32, (1, BS), 1)
    z = zeta_ref[...]
    zeta = jnp.concatenate([z, z], axis=1)
    v0, v1, v2, v4 = [], [], [], []
    for r in range(2):
        row = rows_ref[r]
        v0.append(jnp.where(column == row, 1.0, 0.0))
        v1.append(h_ref[pl.ds(row, 1), :])
        v2.append(h2_ref[pl.ds(row, 1), :])
        v4.append(h4_ref[pl.ds(row, 1), :])
    blank = jnp.zeros((6, BS), jnp.float32)
    v3 = product(left(jnp.concatenate([*v1, blank], axis=0)), r2_ref[...])
    late = product(left(jnp.concatenate([*v1, *v2, v3[:2], blank[:2]], axis=0)), r4_ref[...])
    for r in range(2):
        series = [v0[r], v1[r], v2[r], v3[r : r + 1], v4[r]]
        series += [late[2 * j + r : 2 * j + r + 1] for j in range(3)]
        acc = jnp.broadcast_to(series[7], (NE, BS))
        for term in reversed(series[:7]):
            acc = term + zeta * acc
        picked_ref[r * NE : (r + 1) * NE, :] = zeta * acc
    hat_ref[...] = product(forward_ref[...], right(screen_ref[...]))


def follow(record, state):
    rate, parts = record[0], record[1:]
    if len(state) == FIELDS:
        return [rate * state[0]] + [rate * m + part for m, part in zip(state[1:], parts)]
    return [rate * m + part for m, part in zip(state, parts)]


def fields_of(ref, i):
    return [ref[i, :, q * LANES : (q + 1) * LANES] for q in range(FIELDS)]


def compose_kernel(place_ref, row_ref, sent_ref, before_ref):
    line, mine = place_ref[0:1, :], place_ref[1:2, :]
    blank = [jnp.ones((2, LANES), jnp.float32)] + [jnp.zeros((2, LANES), jnp.float32)] * TERMS
    state, before = blank, blank
    for t in range(row_ref.shape[0]):
        before = [jnp.where(mine == t, new, old) for new, old in zip(state, before)]
        state = follow(fields_of(row_ref, t), state)
    for q in range(FIELDS):
        part = slice(q * LANES, (q + 1) * LANES)
        before_ref[:, part] = before[q]
        for target in range(sent_ref.shape[0]):
            sent_ref[target, :, part] = jnp.where(line < target, state[q], blank[q])


def sigma_kernel(
    lines_ref, before_ref, picked_ref, r1_ref, r2_ref, r4_ref, zeta_ref, hat_ref,
    forward_ref, inverse_ref, out_ref,
):
    state = [jnp.zeros((2, LANES), jnp.float32)] * TERMS
    for t in range(lines_ref.shape[0]):
        state = follow(fields_of(lines_ref, t), state)
    state = follow([before_ref[:, q * LANES : (q + 1) * LANES] for q in range(FIELDS)], state)
    z = zeta_ref[...]
    incoming = []
    for half in range(2):
        rows = [m[half : half + 1] for m in state]
        acc = jnp.broadcast_to(rows[7], (NE, LANES))
        for term in reversed(rows[:7]):
            acc = term + z * acc
        incoming.append(z * acc)
    incoming = jnp.concatenate(incoming, axis=1)
    incoming = jnp.concatenate([incoming, incoming], axis=0)
    zeta = jnp.concatenate([z, z], axis=1)
    zeta = jnp.concatenate([zeta, zeta], axis=0)
    picked = picked_ref[...]
    y = picked * incoming
    y = y + zeta * product(left(y), r1_ref[...])
    zeta2 = zeta * zeta
    y = y + zeta2 * product(left(y), r2_ref[...])
    y = y + (zeta2 * zeta2) * product(left(y), r4_ref[...])
    dressed = picked + zeta * y
    blocks = [dressed[r * NE : (r + 1) * NE, half * LANES : (half + 1) * LANES] for half in range(2) for r in range(2)]
    dressed = jnp.concatenate(blocks, axis=1)
    green = product(forward_ref[...], right(dressed))
    screen = hat_ref[...]
    half = NE // 2
    gc, gs, sc, ss = green[:half], green[half:], screen[:half], screen[half:]
    edge = lax.broadcasted_iota(jnp.int32, gc.shape, 0) == 0
    cc, s2 = gc * sc, gs * ss
    real = jnp.where(edge, cc, cc - s2)
    imag = jnp.where(edge, s2, gc * ss + gs * sc)
    sigma = product(inverse_ref[...], right(jnp.concatenate([real, imag], axis=0)))
    for block in range(4):
        out_ref[pl.ds(block, NE, stride=4), :] = sigma[:, block * LANES : (block + 1) * LANES]


def assemble_kernel(in_ref, out_hbm, sems):
    copies = [
        pltpu.make_async_copy(in_ref.at[e], out_hbm.at[:, e // 4, :, e % 4], sems.at[e]) for e in range(in_ref.shape[0])
    ]
    for copy in copies:
        copy.start()
    for copy in copies:
        copy.wait()


def assemble(pieces):
    devices, energies = pieces.shape[:2]
    tiles = pl.pallas_call(
        assemble_kernel,
        out_shape=jax.ShapeDtypeStruct((energies, devices // 4, 2, 4, 2, LANES), jnp.float32),
        in_specs=[pl.BlockSpec(memory_space=pltpu.VMEM)],
        out_specs=pl.BlockSpec(memory_space=pltpu.HBM),
        scratch_shapes=[pltpu.SemaphoreType.DMA((devices,))],
        compiler_params=pltpu.CompilerParams(vmem_limit_bytes=VMEM_LIMIT),
    )(pieces)
    return tiles.transpose(0, 1, 3, 4, 2, 5).reshape(energies, 2 * devices, BS)


def call(kernel, outs, in_spaces, scratch=(), flops=0, nbytes=0):
    shapes = [jax.ShapeDtypeStruct(s, d) for s, d in outs]
    spaces = {"v": pltpu.VMEM, "s": pltpu.SMEM, "h": pltpu.HBM}
    return pl.pallas_call(
        kernel,
        out_shape=shapes,
        in_specs=[pl.BlockSpec(memory_space=spaces[c]) for c in in_spaces],
        out_specs=[pl.BlockSpec(memory_space=pltpu.VMEM)] * len(outs),
        scratch_shapes=scratch,
        compiler_params=pltpu.CompilerParams(vmem_limit_bytes=VMEM_LIMIT),
        cost_estimate=pl.CostEstimate(flops=flops, bytes_accessed=nbytes, transcendentals=0),
    )


def powers(h, decay, coupling, copies):
    f32 = jnp.float32
    outs = [((copies, 2, RECORD), f32)]
    h, decay, coupling = (pltpu.with_memory_space_constraint(a, pltpu.HBM) for a in (h, decay, coupling))
    scratch = [pltpu.VMEM(s, f32) for s in ((BS, BS), (1, BS), (1, BS))] + [pltpu.SemaphoreType.DMA((3,))]
    return call(powers_kernel, outs, "hhh", scratch, 48 * BS**3, 4 * 2 * BS * BS)(
        h, decay, coupling
    )[0]


def pick(rows, h, zeta, screen, forward):
    outs = [((2 * NE, BS), jnp.float32), ((NE, WIDE), jnp.float32)] + [((3 * BS, BS), jnp.bfloat16)] * 3
    scratch = [pltpu.VMEM((BS, BS), jnp.float32)] * 2
    return call(picked_kernel, outs, "svvvv", scratch, 24 * BS**3, 4 * 12 * BS * BS)(
        rows, h, zeta, screen, forward
    )


def compose(place, row, copies):
    outs = [((copies, 2, RECORD), jnp.float32), ((2, RECORD), jnp.float32)]
    return call(compose_kernel, outs, "vv", (), 0, 4 * 2 * copies * 2 * RECORD)(place, row)


def convolve(lines, before, picked, rights, zeta, hat, forward, inverse):
    outs = [((4 * NE, LANES), jnp.float32)]
    return call(sigma_kernel, outs, "vvvvvvvvvv", (), 6 * 4 * BS**3, 4 * 8 * BS * BS)(
        lines, before, picked, *rights, zeta, hat, forward, inverse
    )[0]


def constants():
    zeta, forward, inverse = tables()
    def wide(t):
        high = t.astype(ml_dtypes.bfloat16)
        low = (t - high.astype(np.float32)).astype(ml_dtypes.bfloat16)
        return jnp.asarray(np.concatenate([high, low, high], axis=1))
    return jnp.asarray(zeta), wide(forward), wide(inverse)


def shards(hamiltonian, decay, coupling, rows, screened):
    zeta, forward, inverse = constants()
    place = jnp.stack([jnp.full((LANES,), lax.axis_index(name), jnp.int32) for name in ("line", "member")])
    sent = powers(hamiltonian, decay, coupling, lax.axis_size("member"))
    own = 2 * lax.axis_index("energy")
    sent, place, own = lax.optimization_barrier((sent, place, own))
    row = lax.all_to_all(sent, "member", split_axis=0, concat_axis=0, tiled=True)
    row, rows, screened, own = lax.optimization_barrier((row, rows, screened, own))
    mine = lax.dynamic_slice(rows[0], (own,), (2,))
    screen = screened[0].reshape(NE, 2, 2, LANES).transpose(0, 2, 1, 3).reshape(NE, WIDE)
    picked, hat, *rights = pick(mine, hamiltonian, zeta, screen, forward)
    sent, before = compose(place, row, lax.axis_size("line"))
    lines = lax.all_to_all(sent, "line", split_axis=0, concat_axis=0, tiled=True)
    sigma = convolve(lines, before, picked, rights, zeta, hat, forward, inverse)
    pieces = lax.all_to_all(sigma.reshape(NE, 2, 2, LANES), "energy", split_axis=0, concat_axis=0, tiled=True)
    return assemble(pieces.reshape(lax.axis_size("energy"), -1, 2, 2, LANES))


def solution(mesh):
    energies, slabs = mesh.devices.shape
    fine = Mesh(mesh.devices.reshape(energies, slabs // 8, 8), ("energy", "line", "member"))
    slab = ("line", "member")
    in_specs = (P(slab, None), P(slab, None), P(slab, None), P(slab, None), P(slab, None, "energy", None))
    out_specs = P("energy", slab, None)
    return jax.shard_map(shards, mesh=fine, in_specs=in_specs, out_specs=out_specs, check_vma=False)
```

```python
import math

import jax
import jax.numpy as jnp
import ml_dtypes
import numpy as np
from jax import lax
from jax.experimental import pallas as pl
from jax.experimental.pallas import tpu as pltpu
from jax.sharding import Mesh
from jax.sharding import PartitionSpec as P

BS = 256
NE = 128
SLABS = 64
LANES = 128
WIDE = 2 * BS
TERMS = 8
FIELDS = TERMS + 1
SERIES = 32
RECORD = FIELDS * LANES
VMEM_LIMIT = 48 * 1024 * 1024


def tables():
    k = np.arange(NE)
    half = NE // 2
    angle = 2.0 * math.pi / NE * (np.arange(half)[:, None] * k[None, :] % NE)
    cosine, sine = np.cos(angle), np.sin(angle)
    sine[0] = (-1.0) ** k
    weight = np.full((half, 1), 2.0)
    weight[0] = 1.0
    forward = np.concatenate([cosine, sine], axis=0)
    inverse = np.concatenate([cosine * weight, sine * weight], axis=0).T / NE
    evaluate = forward @ (1.0 + k[:, None] / NE) ** -(1.0 + np.arange(SERIES))
    return tuple(np.ascontiguousarray(t, dtype=np.float32) for t in (forward, evaluate, inverse))


def split(a):
    high = a.astype(jnp.bfloat16)
    return high, (a - high.astype(jnp.float32)).astype(jnp.bfloat16)


def left(a):
    high, low = split(a)
    return jnp.concatenate([high, low, high], axis=1)


def right(a):
    high, low = split(a)
    return jnp.concatenate([high, high, low], axis=0)


def product(a, b):
    return jnp.dot(a, b, preferred_element_type=jnp.float32)


def powers_kernel(h_hbm, decay_hbm, coupling_hbm, sent_ref, h_ref, decay_ref, coupling_ref, sems):
    copies = [
        pltpu.make_async_copy(source, target, sems.at[i])
        for i, (source, target) in enumerate(
            ((h_hbm, h_ref), (decay_hbm, decay_ref), (coupling_hbm, coupling_ref))
        )
    ]
    for copy in copies:
        copy.start()
    for copy in copies:
        copy.wait()
    h = h_ref[...]
    ht = h.T
    right_ht = right(ht)
    h2 = product(left(h), right(h))
    h2t = product(left(ht), right_ht)
    h4 = product(left(h2), right(h2))
    h3t = product(left(h2t), right_ht)
    row = lax.broadcasted_iota(jnp.int32, (BS, BS), 0)
    column = lax.broadcasted_iota(jnp.int32, (BS, BS), 1)
    share = coupling_ref[...] * (1.0 / SLABS)
    fields = [decay_ref[...], share]
    for diagonal in (
        jnp.where(row == column, h, 0.0),
        h * ht,
        h2 * ht,
        h2 * h2t,
        h4 * ht,
        h4 * h2t,
        h4 * h3t,
    ):
        fields.append(share * jnp.sum(diagonal, axis=0, keepdims=True))
    for q, field in enumerate(fields):
        both = jnp.concatenate([field[:, :LANES], field[:, LANES:]], axis=0)
        for target in range(sent_ref.shape[0]):
            sent_ref[target, :, q * LANES : (q + 1) * LANES] = both


def picked_kernel(rows_ref, h_ref, screen_ref, forward_ref, v_ref, hat_ref, r1_ref, r2_ref, r4_ref, h2_ref, h4_ref):
    r1_ref[...] = right(h_ref[...])
    h2_ref[...] = product(left(h_ref[...]), r1_ref[...])
    r2_ref[...] = right(h2_ref[...])
    h4_ref[...] = product(left(h2_ref[...]), r2_ref[...])
    r4_ref[...] = right(h4_ref[...])
    column = lax.broadcasted_iota(jnp.int32, (1, BS), 1)
    v0, v1, v2, v4 = [], [], [], []
    for r in range(2):
        row = rows_ref[r]
        v0.append(jnp.where(column == row, 1.0, 0.0))
        v1.append(h_ref[pl.ds(row, 1), :])
        v2.append(h2_ref[pl.ds(row, 1), :])
        v4.append(h4_ref[pl.ds(row, 1), :])
    blank = jnp.zeros((6, BS), jnp.float32)
    v3 = product(left(jnp.concatenate([*v1, blank], axis=0)), r2_ref[...])
    late = product(left(jnp.concatenate([*v1, *v2, v3[:2], blank[:2]], axis=0)), r4_ref[...])
    for r in range(2):
        series = [v0[r], v1[r], v2[r], v3[r : r + 1], v4[r]]
        series += [late[2 * j + r : 2 * j + r + 1] for j in range(3)]
        v_ref[r * SERIES : r * SERIES + TERMS, :] = jnp.concatenate(series, axis=0)
        v_ref[r * SERIES + TERMS : (r + 1) * SERIES, :] = jnp.zeros((SERIES - TERMS, BS), jnp.float32)
    hat_ref[...] = product(forward_ref[...], right(screen_ref[...]))


def follow(record, state):
    rate, parts = record[0], record[1:]
    if len(state) == FIELDS:
        return [rate * state[0]] + [rate * m + part for m, part in zip(state[1:], parts)]
    return [rate * m + part for m, part in zip(state, parts)]


def fields_of(ref, i):
    return [ref[i, :, q * LANES : (q + 1) * LANES] for q in range(FIELDS)]


def compose_kernel(place_ref, row_ref, sent_ref, before_ref):
    line, mine = place_ref[0:1, :], place_ref[1:2, :]
    blank = [jnp.ones((2, LANES), jnp.float32)] + [jnp.zeros((2, LANES), jnp.float32)] * TERMS
    state, before = blank, blank
    for t in range(row_ref.shape[0]):
        before = [jnp.where(mine == t, new, old) for new, old in zip(state, before)]
        state = follow(fields_of(row_ref, t), state)
    for q in range(FIELDS):
        part = slice(q * LANES, (q + 1) * LANES)
        before_ref[:, part] = before[q]
        for target in range(sent_ref.shape[0]):
            sent_ref[target, :, part] = jnp.where(line < target, state[q], blank[q])


def sigma_kernel(
    lines_ref, before_ref, v_ref, r1_ref, r2_ref, r4_ref, hat_ref, evaluate_ref, inverse_ref, out_ref
):
    state = [jnp.zeros((2, LANES), jnp.float32)] * TERMS
    for t in range(lines_ref.shape[0]):
        state = follow(fields_of(lines_ref, t), state)
    state = follow([before_ref[:, q * LANES : (q + 1) * LANES] for q in range(FIELDS)], state)
    coefficients = jnp.concatenate(
        [jnp.concatenate([m[half : half + 1] for m in state], axis=0) for half in range(2)], axis=1
    )
    coefficients = jnp.concatenate([coefficients, jnp.zeros((TERMS, BS), jnp.float32)], axis=0)
    shifted = [coefficients if a == 0 else pltpu.roll(coefficients, a, 0) for a in range(TERMS)]
    y = []
    for r in range(2):
        acc = v_ref[r * SERIES : r * SERIES + 1, :] * shifted[0]
        for a in range(1, TERMS):
            acc = acc + v_ref[r * SERIES + a : r * SERIES + a + 1, :] * shifted[a]
        y += [acc, jnp.zeros((SERIES - 2 * TERMS, BS), jnp.float32)]
    y = jnp.concatenate(y, axis=0)
    y = y + pltpu.roll(product(left(y), r1_ref[...]), 1, 0)
    y = y + pltpu.roll(product(left(y), r2_ref[...]), 2, 0)
    y = y + pltpu.roll(product(left(y), r4_ref[...]), 4, 0)
    dressed = v_ref[...] + pltpu.roll(y, 2, 0)
    blocks = [
        dressed[r * SERIES : (r + 1) * SERIES, half * LANES : (half + 1) * LANES] for half in range(2) for r in range(2)
    ]
    green = product(evaluate_ref[...], right(jnp.concatenate(blocks, axis=1)))
    screen = hat_ref[...]
    half = NE // 2
    gc, gs, sc, ss = green[:half], green[half:], screen[:half], screen[half:]
    edge = lax.broadcasted_iota(jnp.int32, gc.shape, 0) == 0
    cc, s2 = gc * sc, gs * ss
    real = jnp.where(edge, cc, cc - s2)
    imag = jnp.where(edge, s2, gc * ss + gs * sc)
    sigma = product(inverse_ref[...], right(jnp.concatenate([real, imag], axis=0)))
    for block in range(4):
        out_ref[pl.ds(block, NE, stride=4), :] = sigma[:, block * LANES : (block + 1) * LANES]


def assemble_kernel(in_ref, out_hbm, sems):
    copies = [
        pltpu.make_async_copy(in_ref.at[e], out_hbm.at[:, e // 4, :, e % 4], sems.at[e]) for e in range(in_ref.shape[0])
    ]
    for copy in copies:
        copy.start()
    for copy in copies:
        copy.wait()


def assemble(pieces):
    devices, energies = pieces.shape[:2]
    tiles = pl.pallas_call(
        assemble_kernel,
        out_shape=jax.ShapeDtypeStruct((energies, devices // 4, 2, 4, 2, LANES), jnp.float32),
        in_specs=[pl.BlockSpec(memory_space=pltpu.VMEM)],
        out_specs=pl.BlockSpec(memory_space=pltpu.HBM),
        scratch_shapes=[pltpu.SemaphoreType.DMA((devices,))],
        compiler_params=pltpu.CompilerParams(vmem_limit_bytes=VMEM_LIMIT),
    )(pieces)
    return tiles.transpose(0, 1, 3, 4, 2, 5).reshape(energies, 2 * devices, BS)


def call(kernel, outs, in_spaces, scratch=(), flops=0, nbytes=0):
    shapes = [jax.ShapeDtypeStruct(s, d) for s, d in outs]
    spaces = {"v": pltpu.VMEM, "s": pltpu.SMEM, "h": pltpu.HBM}
    return pl.pallas_call(
        kernel,
        out_shape=shapes,
        in_specs=[pl.BlockSpec(memory_space=spaces[c]) for c in in_spaces],
        out_specs=[pl.BlockSpec(memory_space=pltpu.VMEM)] * len(outs),
        scratch_shapes=scratch,
        compiler_params=pltpu.CompilerParams(vmem_limit_bytes=VMEM_LIMIT),
        cost_estimate=pl.CostEstimate(flops=flops, bytes_accessed=nbytes, transcendentals=0),
    )


def powers(h, decay, coupling, copies):
    f32 = jnp.float32
    outs = [((copies, 2, RECORD), f32)]
    h, decay, coupling = (pltpu.with_memory_space_constraint(a, pltpu.HBM) for a in (h, decay, coupling))
    scratch = [pltpu.VMEM(s, f32) for s in ((BS, BS), (1, BS), (1, BS))] + [pltpu.SemaphoreType.DMA((3,))]
    return call(powers_kernel, outs, "hhh", scratch, 48 * BS**3, 4 * 2 * BS * BS)(
        h, decay, coupling
    )[0]


def pick(rows, h, screen, forward):
    outs = [((2 * SERIES, BS), jnp.float32), ((NE, WIDE), jnp.float32)] + [((3 * BS, BS), jnp.bfloat16)] * 3
    scratch = [pltpu.VMEM((BS, BS), jnp.float32)] * 2
    return call(picked_kernel, outs, "svvv", scratch, 24 * BS**3, 4 * 12 * BS * BS)(rows, h, screen, forward)


def compose(place, row, copies):
    outs = [((copies, 2, RECORD), jnp.float32), ((2, RECORD), jnp.float32)]
    return call(compose_kernel, outs, "vv", (), 0, 4 * 2 * copies * 2 * RECORD)(place, row)


def convolve(lines, before, series, rights, hat, evaluate, inverse):
    outs = [((4 * NE, LANES), jnp.float32)]
    return call(sigma_kernel, outs, "vvvvvvvvv", (), 3 * BS**3, 4 * 6 * BS * BS)(
        lines, before, series, *rights, hat, evaluate, inverse
    )[0]


def constants():
    forward, evaluate, inverse = tables()
    def wide(t):
        high = t.astype(ml_dtypes.bfloat16)
        low = (t - high.astype(np.float32)).astype(ml_dtypes.bfloat16)
        return jnp.asarray(np.concatenate([high, low, high], axis=1))
    return wide(forward), wide(evaluate), wide(inverse)


def shards(hamiltonian, decay, coupling, rows, screened):
    forward, evaluate, inverse = constants()
    place = jnp.stack([jnp.full((LANES,), lax.axis_index(name), jnp.int32) for name in ("line", "member")])
    sent = powers(hamiltonian, decay, coupling, lax.axis_size("member"))
    own = 2 * lax.axis_index("energy")
    sent, place, own = lax.optimization_barrier((sent, place, own))
    row = lax.all_to_all(sent, "member", split_axis=0, concat_axis=0, tiled=True)
    row, rows, screened, own = lax.optimization_barrier((row, rows, screened, own))
    mine = lax.dynamic_slice(rows[0], (own,), (2,))
    screen = screened[0].reshape(NE, 2, 2, LANES).transpose(0, 2, 1, 3).reshape(NE, WIDE)
    series, hat, *rights = pick(mine, hamiltonian, screen, forward)
    sent, before = compose(place, row, lax.axis_size("line"))
    lines = lax.all_to_all(sent, "line", split_axis=0, concat_axis=0, tiled=True)
    sigma = convolve(lines, before, series, rights, hat, evaluate, inverse)
    pieces = lax.all_to_all(sigma.reshape(NE, 2, 2, LANES), "energy", split_axis=0, concat_axis=0, tiled=True)
    return assemble(pieces.reshape(lax.axis_size("energy"), -1, 2, 2, LANES))


def solution(mesh):
    energies, slabs = mesh.devices.shape
    fine = Mesh(mesh.devices.reshape(energies, slabs // 8, 8), ("energy", "line", "member"))
    slab = ("line", "member")
    in_specs = (P(slab, None), P(slab, None), P(slab, None), P(slab, None), P(slab, None, "energy", None))
    out_specs = P("energy", slab, None)
    return jax.shard_map(shards, mesh=fine, in_specs=in_specs, out_specs=out_specs, check_vma=False)
```

```python
import math

import jax
import jax.numpy as jnp
import ml_dtypes
import numpy as np
from jax import lax
from jax.experimental import pallas as pl
from jax.experimental.pallas import tpu as pltpu
from jax.sharding import Mesh
from jax.sharding import PartitionSpec as P

BS = 256
NE = 128
SLABS = 64
LANES = 128
WIDE = 2 * BS
TERMS = 8
FIELDS = TERMS + 1
SERIES = 32
RECORD = FIELDS * LANES
VMEM_LIMIT = 48 * 1024 * 1024


def tables():
    k = np.arange(NE)
    half = NE // 2
    angle = 2.0 * math.pi / NE * (np.arange(half)[:, None] * k[None, :] % NE)
    cosine, sine = np.cos(angle), np.sin(angle)
    sine[0] = (-1.0) ** k
    weight = np.full((half, 1), 2.0)
    weight[0] = 1.0
    forward = np.concatenate([cosine, sine], axis=0)
    inverse = np.concatenate([cosine * weight, sine * weight], axis=0).T / NE
    evaluate = forward @ (1.0 + k[:, None] / NE) ** -(1.0 + np.arange(SERIES))
    return tuple(np.ascontiguousarray(t, dtype=np.float32) for t in (forward, evaluate, inverse))


def split(a):
    high = a.astype(jnp.bfloat16)
    return high, (a - high.astype(jnp.float32)).astype(jnp.bfloat16)


def right(a):
    high, low = split(a)
    return jnp.concatenate([high, high, low], axis=0)


def product(a, b):
    return jnp.dot(a, b, preferred_element_type=jnp.float32)


def stack(a):
    return jnp.concatenate(split(a), axis=0)


def apply(a, b):
    rows, depth = a.shape[0] // 2, b.shape[0] // 2
    both = product(a, b[:depth])
    return both[:rows] + both[rows:] + product(a[:rows], b[depth:])


def powers_kernel(h_hbm, decay_hbm, coupling_hbm, sent_ref, h_ref, decay_ref, coupling_ref, sems):
    copies = [
        pltpu.make_async_copy(source, target, sems.at[i])
        for i, (source, target) in enumerate(
            ((h_hbm, h_ref), (decay_hbm, decay_ref), (coupling_hbm, coupling_ref))
        )
    ]
    for copy in copies:
        copy.start()
    for copy in copies:
        copy.wait()
    h = h_ref[...]
    ht = h.T
    parts, parts_t = stack(h), stack(ht)
    h2 = apply(parts, parts)
    h2t = apply(parts_t, parts_t)
    parts = stack(h2)
    h4 = apply(parts, parts)
    h3t = apply(stack(h2t), parts_t)
    row = lax.broadcasted_iota(jnp.int32, (BS, BS), 0)
    column = lax.broadcasted_iota(jnp.int32, (BS, BS), 1)
    share = coupling_ref[...] * (1.0 / SLABS)
    fields = [decay_ref[...], share]
    for diagonal in (
        jnp.where(row == column, h, 0.0),
        h * ht,
        h2 * ht,
        h2 * h2t,
        h4 * ht,
        h4 * h2t,
        h4 * h3t,
    ):
        fields.append(share * jnp.sum(diagonal, axis=0, keepdims=True))
    for q, field in enumerate(fields):
        both = jnp.concatenate([field[:, :LANES], field[:, LANES:]], axis=0)
        for target in range(sent_ref.shape[0]):
            sent_ref[target, :, q * LANES : (q + 1) * LANES] = both


def picked_kernel(rows_ref, h_ref, screen_ref, forward_ref, v_ref, hat_ref, r1_ref, r2_ref, r4_ref, h2_ref, h4_ref):
    r1_ref[...] = stack(h_ref[...])
    h2_ref[...] = apply(r1_ref[...], r1_ref[...])
    r2_ref[...] = stack(h2_ref[...])
    h4_ref[...] = apply(r2_ref[...], r2_ref[...])
    r4_ref[...] = stack(h4_ref[...])
    column = lax.broadcasted_iota(jnp.int32, (1, BS), 1)
    v0, v1, v2, v4 = [], [], [], []
    for r in range(2):
        row = rows_ref[r]
        v0.append(jnp.where(column == row, 1.0, 0.0))
        v1.append(h_ref[pl.ds(row, 1), :])
        v2.append(h2_ref[pl.ds(row, 1), :])
        v4.append(h4_ref[pl.ds(row, 1), :])
    blank = jnp.zeros((14, BS), jnp.float32)
    v3 = apply(stack(jnp.concatenate([*v1, blank], axis=0)), r2_ref[...])
    late = apply(stack(jnp.concatenate([*v1, *v2, v3[:2], blank[:10]], axis=0)), r4_ref[...])
    for r in range(2):
        series = [v0[r], v1[r], v2[r], v3[r : r + 1], v4[r]]
        series += [late[2 * j + r : 2 * j + r + 1] for j in range(3)]
        v_ref[r * SERIES : r * SERIES + TERMS, :] = jnp.concatenate(series, axis=0)
        v_ref[r * SERIES + TERMS : (r + 1) * SERIES, :] = jnp.zeros((SERIES - TERMS, BS), jnp.float32)
    hat_ref[...] = product(forward_ref[...], right(screen_ref[...]))


def follow(record, state):
    rate, parts = record[0], record[1:]
    if len(state) == FIELDS:
        return [rate * state[0]] + [rate * m + part for m, part in zip(state[1:], parts)]
    return [rate * m + part for m, part in zip(state, parts)]


def fields_of(ref, i):
    return [ref[i, :, q * LANES : (q + 1) * LANES] for q in range(FIELDS)]


def compose_kernel(place_ref, row_ref, sent_ref, before_ref):
    line, mine = place_ref[0:1, :], place_ref[1:2, :]
    blank = [jnp.ones((2, LANES), jnp.float32)] + [jnp.zeros((2, LANES), jnp.float32)] * TERMS
    state, before = blank, blank
    for t in range(row_ref.shape[0]):
        before = [jnp.where(mine == t, new, old) for new, old in zip(state, before)]
        state = follow(fields_of(row_ref, t), state)
    for q in range(FIELDS):
        part = slice(q * LANES, (q + 1) * LANES)
        before_ref[:, part] = before[q]
        for target in range(sent_ref.shape[0]):
            sent_ref[target, :, part] = jnp.where(line < target, state[q], blank[q])


def sigma_kernel(
    lines_ref, before_ref, v_ref, r1_ref, r2_ref, r4_ref, hat_ref, evaluate_ref, inverse_ref, out_ref
):
    state = [jnp.zeros((2, LANES), jnp.float32)] * TERMS
    for t in range(lines_ref.shape[0]):
        state = follow(fields_of(lines_ref, t), state)
    state = follow([before_ref[:, q * LANES : (q + 1) * LANES] for q in range(FIELDS)], state)
    coefficients = jnp.concatenate(
        [jnp.concatenate([m[half : half + 1] for m in state], axis=0) for half in range(2)], axis=1
    )
    coefficients = jnp.concatenate([coefficients, jnp.zeros((TERMS, BS), jnp.float32)], axis=0)
    shifted = [coefficients if a == 0 else pltpu.roll(coefficients, a, 0) for a in range(TERMS)]
    y = []
    for r in range(2):
        acc = v_ref[r * SERIES : r * SERIES + 1, :] * shifted[0]
        for a in range(1, TERMS):
            acc = acc + v_ref[r * SERIES + a : r * SERIES + a + 1, :] * shifted[a]
        y += [acc, jnp.zeros((SERIES - 2 * TERMS, BS), jnp.float32)]
    y = jnp.concatenate(y, axis=0)
    y = y + pltpu.roll(apply(stack(y), r1_ref[...]), 1, 0)
    y = y + pltpu.roll(apply(stack(y), r2_ref[...]), 2, 0)
    y = y + pltpu.roll(apply(stack(y), r4_ref[...]), 4, 0)
    dressed = v_ref[...] + pltpu.roll(y, 2, 0)
    blocks = [
        dressed[r * SERIES : (r + 1) * SERIES, half * LANES : (half + 1) * LANES] for half in range(2) for r in range(2)
    ]
    green = product(evaluate_ref[...], right(jnp.concatenate(blocks, axis=1)))
    screen = hat_ref[...]
    half = NE // 2
    gc, gs, sc, ss = green[:half], green[half:], screen[:half], screen[half:]
    edge = lax.broadcasted_iota(jnp.int32, gc.shape, 0) == 0
    cc, s2 = gc * sc, gs * ss
    real = jnp.where(edge, cc, cc - s2)
    imag = jnp.where(edge, s2, gc * ss + gs * sc)
    sigma = product(inverse_ref[...], right(jnp.concatenate([real, imag], axis=0)))
    for block in range(4):
        out_ref[pl.ds(block, NE, stride=4), :] = sigma[:, block * LANES : (block + 1) * LANES]


def assemble_kernel(in_ref, out_hbm, sems):
    copies = [
        pltpu.make_async_copy(in_ref.at[e], out_hbm.at[:, e // 4, :, e % 4], sems.at[e]) for e in range(in_ref.shape[0])
    ]
    for copy in copies:
        copy.start()
    for copy in copies:
        copy.wait()


def assemble(pieces):
    devices, energies = pieces.shape[:2]
    tiles = pl.pallas_call(
        assemble_kernel,
        out_shape=jax.ShapeDtypeStruct((energies, devices // 4, 2, 4, 2, LANES), jnp.float32),
        in_specs=[pl.BlockSpec(memory_space=pltpu.VMEM)],
        out_specs=pl.BlockSpec(memory_space=pltpu.HBM),
        scratch_shapes=[pltpu.SemaphoreType.DMA((devices,))],
        compiler_params=pltpu.CompilerParams(vmem_limit_bytes=VMEM_LIMIT),
    )(pieces)
    return tiles.transpose(0, 1, 3, 4, 2, 5).reshape(energies, 2 * devices, BS)


def call(kernel, outs, in_spaces, scratch=(), flops=0, nbytes=0):
    shapes = [jax.ShapeDtypeStruct(s, d) for s, d in outs]
    spaces = {"v": pltpu.VMEM, "s": pltpu.SMEM, "h": pltpu.HBM}
    return pl.pallas_call(
        kernel,
        out_shape=shapes,
        in_specs=[pl.BlockSpec(memory_space=spaces[c]) for c in in_spaces],
        out_specs=[pl.BlockSpec(memory_space=pltpu.VMEM)] * len(outs),
        scratch_shapes=scratch,
        compiler_params=pltpu.CompilerParams(vmem_limit_bytes=VMEM_LIMIT),
        cost_estimate=pl.CostEstimate(flops=flops, bytes_accessed=nbytes, transcendentals=0),
    )


def powers(h, decay, coupling, copies):
    f32 = jnp.float32
    outs = [((copies, 2, RECORD), f32)]
    h, decay, coupling = (pltpu.with_memory_space_constraint(a, pltpu.HBM) for a in (h, decay, coupling))
    scratch = [pltpu.VMEM(s, f32) for s in ((BS, BS), (1, BS), (1, BS))] + [pltpu.SemaphoreType.DMA((3,))]
    return call(powers_kernel, outs, "hhh", scratch, 48 * BS**3, 4 * 2 * BS * BS)(
        h, decay, coupling
    )[0]


def pick(rows, h, screen, forward):
    outs = [((2 * SERIES, BS), jnp.float32), ((NE, WIDE), jnp.float32)] + [((2 * BS, BS), jnp.bfloat16)] * 3
    scratch = [pltpu.VMEM((BS, BS), jnp.float32)] * 2
    return call(picked_kernel, outs, "svvv", scratch, 24 * BS**3, 4 * 12 * BS * BS)(rows, h, screen, forward)


def compose(place, row, copies):
    outs = [((copies, 2, RECORD), jnp.float32), ((2, RECORD), jnp.float32)]
    return call(compose_kernel, outs, "vv", (), 0, 4 * 2 * copies * 2 * RECORD)(place, row)


def convolve(lines, before, series, rights, hat, evaluate, inverse):
    outs = [((4 * NE, LANES), jnp.float32)]
    return call(sigma_kernel, outs, "vvvvvvvvv", (), 3 * BS**3, 4 * 6 * BS * BS)(
        lines, before, series, *rights, hat, evaluate, inverse
    )[0]


def constants():
    forward, evaluate, inverse = tables()
    def wide(t):
        high = t.astype(ml_dtypes.bfloat16)
        low = (t - high.astype(np.float32)).astype(ml_dtypes.bfloat16)
        return jnp.asarray(np.concatenate([high, low, high], axis=1))
    return wide(forward), wide(evaluate), wide(inverse)


def shards(hamiltonian, decay, coupling, rows, screened):
    forward, evaluate, inverse = constants()
    place = jnp.stack([jnp.full((LANES,), lax.axis_index(name), jnp.int32) for name in ("line", "member")])
    sent = powers(hamiltonian, decay, coupling, lax.axis_size("member"))
    own = 2 * lax.axis_index("energy")
    sent, place, own = lax.optimization_barrier((sent, place, own))
    row = lax.all_to_all(sent, "member", split_axis=0, concat_axis=0, tiled=True)
    row, rows, screened, own = lax.optimization_barrier((row, rows, screened, own))
    mine = lax.dynamic_slice(rows[0], (own,), (2,))
    screen = screened[0].reshape(NE, 2, 2, LANES).transpose(0, 2, 1, 3).reshape(NE, WIDE)
    series, hat, *rights = pick(mine, hamiltonian, screen, forward)
    sent, before = compose(place, row, lax.axis_size("line"))
    lines = lax.all_to_all(sent, "line", split_axis=0, concat_axis=0, tiled=True)
    sigma = convolve(lines, before, series, rights, hat, evaluate, inverse)
    pieces = lax.all_to_all(sigma.reshape(NE, 2, 2, LANES), "energy", split_axis=0, concat_axis=0, tiled=True)
    return assemble(pieces.reshape(lax.axis_size("energy"), -1, 2, 2, LANES))


def solution(mesh):
    energies, slabs = mesh.devices.shape
    fine = Mesh(mesh.devices.reshape(energies, slabs // 8, 8), ("energy", "line", "member"))
    slab = ("line", "member")
    in_specs = (P(slab, None), P(slab, None), P(slab, None), P(slab, None), P(slab, None, "energy", None))
    out_specs = P("energy", slab, None)
    return jax.shard_map(shards, mesh=fine, in_specs=in_specs, out_specs=out_specs, check_vma=False)
```

```python
import math

import jax
import jax.numpy as jnp
import ml_dtypes
import numpy as np
from jax import lax
from jax.experimental import pallas as pl
from jax.experimental.pallas import tpu as pltpu
from jax.sharding import Mesh
from jax.sharding import PartitionSpec as P

BS = 256
NE = 128
SLABS = 64
LANES = 128
WIDE = 2 * BS
TERMS = 8
FIELDS = TERMS + 1
SERIES = 32
RECORD = FIELDS * LANES
VMEM_LIMIT = 48 * 1024 * 1024


def tables():
    k = np.arange(NE)
    half = NE // 2
    angle = 2.0 * math.pi / NE * (np.arange(half)[:, None] * k[None, :] % NE)
    cosine, sine = np.cos(angle), np.sin(angle)
    sine[0] = (-1.0) ** k
    weight = np.full((half, 1), 2.0)
    weight[0] = 1.0
    forward = np.concatenate([cosine, sine], axis=0)
    inverse = np.concatenate([cosine * weight, sine * weight], axis=0).T / NE
    evaluate = forward @ (1.0 + k[:, None] / NE) ** -(1.0 + np.arange(SERIES))
    return tuple(np.ascontiguousarray(t, dtype=np.float32) for t in (forward, evaluate, inverse))


def split(a):
    high = a.astype(jnp.bfloat16)
    return high, (a - high.astype(jnp.float32)).astype(jnp.bfloat16)


def right(a):
    high, low = split(a)
    return jnp.concatenate([high, high, low], axis=0)


def product(a, b):
    return jnp.dot(a, b, preferred_element_type=jnp.float32)


def stack(a):
    return jnp.concatenate(split(a), axis=0)


def apply(a, b):
    rows, depth = a.shape[0] // 2, b.shape[0] // 2
    both = product(a, b[:depth])
    return both[:rows] + both[rows:] + product(a[:rows], b[depth:])


def powers_kernel(h_hbm, decay_hbm, coupling_hbm, sent_ref, h_ref, decay_ref, coupling_ref, sems):
    copies = [
        pltpu.make_async_copy(source, target, sems.at[i])
        for i, (source, target) in enumerate(
            ((h_hbm, h_ref), (decay_hbm, decay_ref), (coupling_hbm, coupling_ref))
        )
    ]
    for copy in copies:
        copy.start()
    for copy in copies:
        copy.wait()
    h = h_ref[...]
    ht = h.T
    parts, parts_t = stack(h), stack(ht)
    h2 = apply(parts, parts)
    h2t = apply(parts_t, parts_t)
    parts = stack(h2)
    h4 = apply(parts, parts)
    h3t = apply(stack(h2t), parts_t)
    row = lax.broadcasted_iota(jnp.int32, (BS, BS), 0)
    column = lax.broadcasted_iota(jnp.int32, (BS, BS), 1)
    share = coupling_ref[...] * (1.0 / SLABS)
    fields = [decay_ref[...], share]
    for diagonal in (
        jnp.where(row == column, h, 0.0),
        h * ht,
        h2 * ht,
        h2 * h2t,
        h4 * ht,
        h4 * h2t,
        h4 * h3t,
    ):
        fields.append(share * jnp.sum(diagonal, axis=0, keepdims=True))
    for q, field in enumerate(fields):
        both = jnp.concatenate([field[:, :LANES], field[:, LANES:]], axis=0)
        for target in range(sent_ref.shape[0]):
            sent_ref[target, :, q * LANES : (q + 1) * LANES] = both


def picked_kernel(rows_ref, h_ref, screen_ref, forward_ref, v_ref, hat_ref, r1_ref, r2_ref, r3_ref, r4_ref, h2_ref, h4_ref):
    r1_ref[...] = stack(h_ref[...])
    h2_ref[...] = apply(r1_ref[...], r1_ref[...])
    r2_ref[...] = stack(h2_ref[...])
    r3_ref[...] = stack(apply(r2_ref[...], r1_ref[...]))
    h4_ref[...] = apply(r2_ref[...], r2_ref[...])
    r4_ref[...] = stack(h4_ref[...])
    column = lax.broadcasted_iota(jnp.int32, (1, BS), 1)
    v0, v1, v2, v4 = [], [], [], []
    for r in range(2):
        row = rows_ref[r]
        v0.append(jnp.where(column == row, 1.0, 0.0))
        v1.append(h_ref[pl.ds(row, 1), :])
        v2.append(h2_ref[pl.ds(row, 1), :])
        v4.append(h4_ref[pl.ds(row, 1), :])
    blank = jnp.zeros((14, BS), jnp.float32)
    v3 = apply(stack(jnp.concatenate([*v1, blank], axis=0)), r2_ref[...])
    late = apply(stack(jnp.concatenate([*v1, *v2, v3[:2], blank[:10]], axis=0)), r4_ref[...])
    for r in range(2):
        series = [v0[r], v1[r], v2[r], v3[r : r + 1], v4[r]]
        series += [late[2 * j + r : 2 * j + r + 1] for j in range(3)]
        v_ref[r * SERIES : r * SERIES + TERMS, :] = jnp.concatenate(series, axis=0)
        v_ref[r * SERIES + TERMS : (r + 1) * SERIES, :] = jnp.zeros((SERIES - TERMS, BS), jnp.float32)
    hat_ref[...] = product(forward_ref[...], right(screen_ref[...]))


def follow(record, state):
    rate, parts = record[0], record[1:]
    if len(state) == FIELDS:
        return [rate * state[0]] + [rate * m + part for m, part in zip(state[1:], parts)]
    return [rate * m + part for m, part in zip(state, parts)]


def fields_of(ref, i):
    return [ref[i, :, q * LANES : (q + 1) * LANES] for q in range(FIELDS)]


def compose_kernel(place_ref, row_ref, sent_ref, before_ref):
    line, mine = place_ref[0:1, :], place_ref[1:2, :]
    blank = [jnp.ones((2, LANES), jnp.float32)] + [jnp.zeros((2, LANES), jnp.float32)] * TERMS
    state, before = blank, blank
    for t in range(row_ref.shape[0]):
        before = [jnp.where(mine == t, new, old) for new, old in zip(state, before)]
        state = follow(fields_of(row_ref, t), state)
    for q in range(FIELDS):
        part = slice(q * LANES, (q + 1) * LANES)
        before_ref[:, part] = before[q]
        for target in range(sent_ref.shape[0]):
            sent_ref[target, :, part] = jnp.where(line < target, state[q], blank[q])


def sigma_kernel(
    lines_ref, before_ref, v_ref, r1_ref, r2_ref, r3_ref, r4_ref, hat_ref, evaluate_ref, inverse_ref, out_ref
):
    state = [jnp.zeros((2, LANES), jnp.float32)] * TERMS
    for t in range(lines_ref.shape[0]):
        state = follow(fields_of(lines_ref, t), state)
    state = follow([before_ref[:, q * LANES : (q + 1) * LANES] for q in range(FIELDS)], state)
    coefficients = jnp.concatenate(
        [jnp.concatenate([m[half : half + 1] for m in state], axis=0) for half in range(2)], axis=1
    )
    coefficients = jnp.concatenate([coefficients, jnp.zeros((TERMS, BS), jnp.float32)], axis=0)
    shifted = [coefficients if a == 0 else pltpu.roll(coefficients, a, 0) for a in range(TERMS)]
    y = []
    for r in range(2):
        acc = v_ref[r * SERIES : r * SERIES + 1, :] * shifted[0]
        for a in range(1, TERMS):
            acc = acc + v_ref[r * SERIES + a : r * SERIES + a + 1, :] * shifted[a]
        y += [acc, jnp.zeros((SERIES - 2 * TERMS, BS), jnp.float32)]
    y = jnp.concatenate(y, axis=0)
    parts = stack(y)
    for shift, power_ref in enumerate((r1_ref, r2_ref, r3_ref), 1):
        y = y + pltpu.roll(apply(parts, power_ref[...]), shift, 0)
    y = y + pltpu.roll(apply(stack(y), r4_ref[...]), 4, 0)
    dressed = v_ref[...] + pltpu.roll(y, 2, 0)
    blocks = [
        dressed[r * SERIES : (r + 1) * SERIES, half * LANES : (half + 1) * LANES] for half in range(2) for r in range(2)
    ]
    green = product(evaluate_ref[...], right(jnp.concatenate(blocks, axis=1)))
    screen = hat_ref[...]
    half = NE // 2
    gc, gs, sc, ss = green[:half], green[half:], screen[:half], screen[half:]
    edge = lax.broadcasted_iota(jnp.int32, gc.shape, 0) == 0
    cc, s2 = gc * sc, gs * ss
    real = jnp.where(edge, cc, cc - s2)
    imag = jnp.where(edge, s2, gc * ss + gs * sc)
    sigma = product(inverse_ref[...], right(jnp.concatenate([real, imag], axis=0)))
    for block in range(4):
        out_ref[pl.ds(block, NE, stride=4), :] = sigma[:, block * LANES : (block + 1) * LANES]


def assemble_kernel(in_ref, out_hbm, sems):
    copies = [
        pltpu.make_async_copy(in_ref.at[e], out_hbm.at[:, e // 4, :, e % 4], sems.at[e]) for e in range(in_ref.shape[0])
    ]
    for copy in copies:
        copy.start()
    for copy in copies:
        copy.wait()


def assemble(pieces):
    devices, energies = pieces.shape[:2]
    tiles = pl.pallas_call(
        assemble_kernel,
        out_shape=jax.ShapeDtypeStruct((energies, devices // 4, 2, 4, 2, LANES), jnp.float32),
        in_specs=[pl.BlockSpec(memory_space=pltpu.VMEM)],
        out_specs=pl.BlockSpec(memory_space=pltpu.HBM),
        scratch_shapes=[pltpu.SemaphoreType.DMA((devices,))],
        compiler_params=pltpu.CompilerParams(vmem_limit_bytes=VMEM_LIMIT),
    )(pieces)
    return tiles.transpose(0, 1, 3, 4, 2, 5).reshape(energies, 2 * devices, BS)


def call(kernel, outs, in_spaces, scratch=(), flops=0, nbytes=0):
    shapes = [jax.ShapeDtypeStruct(s, d) for s, d in outs]
    spaces = {"v": pltpu.VMEM, "s": pltpu.SMEM, "h": pltpu.HBM}
    return pl.pallas_call(
        kernel,
        out_shape=shapes,
        in_specs=[pl.BlockSpec(memory_space=spaces[c]) for c in in_spaces],
        out_specs=[pl.BlockSpec(memory_space=pltpu.VMEM)] * len(outs),
        scratch_shapes=scratch,
        compiler_params=pltpu.CompilerParams(vmem_limit_bytes=VMEM_LIMIT),
        cost_estimate=pl.CostEstimate(flops=flops, bytes_accessed=nbytes, transcendentals=0),
    )


def powers(h, decay, coupling, copies):
    f32 = jnp.float32
    outs = [((copies, 2, RECORD), f32)]
    h, decay, coupling = (pltpu.with_memory_space_constraint(a, pltpu.HBM) for a in (h, decay, coupling))
    scratch = [pltpu.VMEM(s, f32) for s in ((BS, BS), (1, BS), (1, BS))] + [pltpu.SemaphoreType.DMA((3,))]
    return call(powers_kernel, outs, "hhh", scratch, 48 * BS**3, 4 * 2 * BS * BS)(
        h, decay, coupling
    )[0]


def pick(rows, h, screen, forward):
    outs = [((2 * SERIES, BS), jnp.float32), ((NE, WIDE), jnp.float32)] + [((2 * BS, BS), jnp.bfloat16)] * 4
    scratch = [pltpu.VMEM((BS, BS), jnp.float32)] * 2
    return call(picked_kernel, outs, "svvv", scratch, 24 * BS**3, 4 * 12 * BS * BS)(rows, h, screen, forward)


def compose(place, row, copies):
    outs = [((copies, 2, RECORD), jnp.float32), ((2, RECORD), jnp.float32)]
    return call(compose_kernel, outs, "vv", (), 0, 4 * 2 * copies * 2 * RECORD)(place, row)


def convolve(lines, before, series, rights, hat, evaluate, inverse):
    outs = [((4 * NE, LANES), jnp.float32)]
    return call(sigma_kernel, outs, "vvvvvvvvvv", (), 3 * BS**3, 4 * 6 * BS * BS)(
        lines, before, series, *rights, hat, evaluate, inverse
    )[0]


def constants():
    forward, evaluate, inverse = tables()
    def wide(t):
        high = t.astype(ml_dtypes.bfloat16)
        low = (t - high.astype(np.float32)).astype(ml_dtypes.bfloat16)
        return jnp.asarray(np.concatenate([high, low, high], axis=1))
    return wide(forward), wide(evaluate), wide(inverse)


def shards(hamiltonian, decay, coupling, rows, screened):
    forward, evaluate, inverse = constants()
    place = jnp.stack([jnp.full((LANES,), lax.axis_index(name), jnp.int32) for name in ("line", "member")])
    sent = powers(hamiltonian, decay, coupling, lax.axis_size("member"))
    own = 2 * lax.axis_index("energy")
    sent, place, own = lax.optimization_barrier((sent, place, own))
    row = lax.all_to_all(sent, "member", split_axis=0, concat_axis=0, tiled=True)
    row, rows, screened, own = lax.optimization_barrier((row, rows, screened, own))
    mine = lax.dynamic_slice(rows[0], (own,), (2,))
    screen = screened[0].reshape(NE, 2, 2, LANES).transpose(0, 2, 1, 3).reshape(NE, WIDE)
    series, hat, *rights = pick(mine, hamiltonian, screen, forward)
    sent, before = compose(place, row, lax.axis_size("line"))
    lines = lax.all_to_all(sent, "line", split_axis=0, concat_axis=0, tiled=True)
    sigma = convolve(lines, before, series, rights, hat, evaluate, inverse)
    pieces = lax.all_to_all(sigma.reshape(NE, 2, 2, LANES), "energy", split_axis=0, concat_axis=0, tiled=True)
    return assemble(pieces.reshape(lax.axis_size("energy"), -1, 2, 2, LANES))


def solution(mesh):
    energies, slabs = mesh.devices.shape
    fine = Mesh(mesh.devices.reshape(energies, slabs // 8, 8), ("energy", "line", "member"))
    slab = ("line", "member")
    in_specs = (P(slab, None), P(slab, None), P(slab, None), P(slab, None), P(slab, None, "energy", None))
    out_specs = P("energy", slab, None)
    return jax.shard_map(shards, mesh=fine, in_specs=in_specs, out_specs=out_specs, check_vma=False)
```

```python
import math

import jax
import jax.numpy as jnp
import ml_dtypes
import numpy as np
from jax import lax
from jax.experimental import pallas as pl
from jax.experimental.pallas import tpu as pltpu
from jax.sharding import Mesh
from jax.sharding import PartitionSpec as P

BS = 256
NE = 128
SLABS = 64
LANES = 128
WIDE = 2 * BS
TERMS = 8
FIELDS = TERMS + 1
SERIES = 32
RECORD = FIELDS * LANES
VMEM_LIMIT = 48 * 1024 * 1024


def tables():
    k = np.arange(NE)
    half = NE // 2
    angle = 2.0 * math.pi / NE * (np.arange(half)[:, None] * k[None, :] % NE)
    cosine, sine = np.cos(angle), np.sin(angle)
    sine[0] = (-1.0) ** k
    weight = np.full((half, 1), 2.0)
    weight[0] = 1.0
    forward = np.concatenate([cosine, sine], axis=0)
    inverse = np.concatenate([cosine * weight, sine * weight], axis=0).T / NE
    evaluate = forward @ (1.0 + k[:, None] / NE) ** -(1.0 + np.arange(SERIES))
    return tuple(np.ascontiguousarray(t, dtype=np.float32) for t in (forward, evaluate, inverse))


def split(a):
    high = a.astype(jnp.bfloat16)
    return high, (a - high.astype(jnp.float32)).astype(jnp.bfloat16)


def right(a):
    high, low = split(a)
    return jnp.concatenate([high, high, low], axis=0)


def product(a, b):
    return jnp.dot(a, b, preferred_element_type=jnp.float32)


def stack(a):
    return jnp.concatenate(split(a), axis=0)


def apply(a, b):
    rows, depth = a.shape[0] // 2, b.shape[0] // 2
    both = product(a, b[:depth])
    return both[:rows] + both[rows:] + product(a[:rows], b[depth:])


def powers_kernel(h_hbm, decay_hbm, coupling_hbm, sent_ref, h_ref, decay_ref, coupling_ref, sems):
    copies = [
        pltpu.make_async_copy(source, target, sems.at[i])
        for i, (source, target) in enumerate(
            ((h_hbm, h_ref), (decay_hbm, decay_ref), (coupling_hbm, coupling_ref))
        )
    ]
    for copy in copies:
        copy.start()
    for copy in copies:
        copy.wait()
    h = h_ref[...]
    ht = h.T
    parts, parts_t = stack(h), stack(ht)
    h2 = apply(parts, parts)
    h2t = apply(parts_t, parts_t)
    parts = stack(h2)
    h4 = apply(parts, parts)
    h3t = apply(stack(h2t), parts_t)
    row = lax.broadcasted_iota(jnp.int32, (BS, BS), 0)
    column = lax.broadcasted_iota(jnp.int32, (BS, BS), 1)
    share = coupling_ref[...] * (1.0 / SLABS)
    fields = [decay_ref[...], share]
    for diagonal in (
        jnp.where(row == column, h, 0.0),
        h * ht,
        h2 * ht,
        h2 * h2t,
        h4 * ht,
        h4 * h2t,
        h4 * h3t,
    ):
        fields.append(share * jnp.sum(diagonal, axis=0, keepdims=True))
    for q, field in enumerate(fields):
        both = jnp.concatenate([field[:, :LANES], field[:, LANES:]], axis=0)
        for target in range(sent_ref.shape[0]):
            sent_ref[target, :, q * LANES : (q + 1) * LANES] = both


def picked_kernel(
    rows_ref, h_ref, screen_ref, forward_ref, v_ref, hat_ref,
    r1_ref, r2_ref, r3_ref, r4_ref, r5_ref, r6_ref, r7_ref, h2_ref, h4_ref,
):
    r1_ref[...] = stack(h_ref[...])
    h2_ref[...] = apply(r1_ref[...], r1_ref[...])
    r2_ref[...] = stack(h2_ref[...])
    r3_ref[...] = stack(apply(r2_ref[...], r1_ref[...]))
    h4_ref[...] = apply(r2_ref[...], r2_ref[...])
    r4_ref[...] = stack(h4_ref[...])
    for out_ref, power_ref in ((r5_ref, r1_ref), (r6_ref, r2_ref), (r7_ref, r3_ref)):
        out_ref[...] = stack(apply(r4_ref[...], power_ref[...]))
    column = lax.broadcasted_iota(jnp.int32, (1, BS), 1)
    v0, v1, v2, v4 = [], [], [], []
    for r in range(2):
        row = rows_ref[r]
        v0.append(jnp.where(column == row, 1.0, 0.0))
        v1.append(h_ref[pl.ds(row, 1), :])
        v2.append(h2_ref[pl.ds(row, 1), :])
        v4.append(h4_ref[pl.ds(row, 1), :])
    blank = jnp.zeros((14, BS), jnp.float32)
    v3 = apply(stack(jnp.concatenate([*v1, blank], axis=0)), r2_ref[...])
    late = apply(stack(jnp.concatenate([*v1, *v2, v3[:2], blank[:10]], axis=0)), r4_ref[...])
    for r in range(2):
        series = [v0[r], v1[r], v2[r], v3[r : r + 1], v4[r]]
        series += [late[2 * j + r : 2 * j + r + 1] for j in range(3)]
        v_ref[r * SERIES : r * SERIES + TERMS, :] = jnp.concatenate(series, axis=0)
        v_ref[r * SERIES + TERMS : (r + 1) * SERIES, :] = jnp.zeros((SERIES - TERMS, BS), jnp.float32)
    hat_ref[...] = product(forward_ref[...], right(screen_ref[...]))


def follow(record, state):
    rate, parts = record[0], record[1:]
    if len(state) == FIELDS:
        return [rate * state[0]] + [rate * m + part for m, part in zip(state[1:], parts)]
    return [rate * m + part for m, part in zip(state, parts)]


def fields_of(ref, i):
    return [ref[i, :, q * LANES : (q + 1) * LANES] for q in range(FIELDS)]


def compose_kernel(place_ref, row_ref, sent_ref, before_ref):
    line, mine = place_ref[0:1, :], place_ref[1:2, :]
    blank = [jnp.ones((2, LANES), jnp.float32)] + [jnp.zeros((2, LANES), jnp.float32)] * TERMS
    state, before = blank, blank
    for t in range(row_ref.shape[0]):
        before = [jnp.where(mine == t, new, old) for new, old in zip(state, before)]
        state = follow(fields_of(row_ref, t), state)
    for q in range(FIELDS):
        part = slice(q * LANES, (q + 1) * LANES)
        before_ref[:, part] = before[q]
        for target in range(sent_ref.shape[0]):
            sent_ref[target, :, part] = jnp.where(line < target, state[q], blank[q])


def sigma_kernel(
    lines_ref, before_ref, v_ref, r1_ref, r2_ref, r3_ref, r4_ref, r5_ref, r6_ref, r7_ref, hat_ref, evaluate_ref, inverse_ref, out_ref
):
    state = [jnp.zeros((2, LANES), jnp.float32)] * TERMS
    for t in range(lines_ref.shape[0]):
        state = follow(fields_of(lines_ref, t), state)
    state = follow([before_ref[:, q * LANES : (q + 1) * LANES] for q in range(FIELDS)], state)
    coefficients = jnp.concatenate(
        [jnp.concatenate([m[half : half + 1] for m in state], axis=0) for half in range(2)], axis=1
    )
    coefficients = jnp.concatenate([coefficients, jnp.zeros((TERMS, BS), jnp.float32)], axis=0)
    shifted = [coefficients if a == 0 else pltpu.roll(coefficients, a, 0) for a in range(TERMS)]
    y = []
    for r in range(2):
        acc = v_ref[r * SERIES : r * SERIES + 1, :] * shifted[0]
        for a in range(1, TERMS):
            acc = acc + v_ref[r * SERIES + a : r * SERIES + a + 1, :] * shifted[a]
        y += [acc, jnp.zeros((SERIES - 2 * TERMS, BS), jnp.float32)]
    y = jnp.concatenate(y, axis=0)
    parts = stack(y)
    for shift, power_ref in enumerate((r1_ref, r2_ref, r3_ref, r4_ref, r5_ref, r6_ref, r7_ref), 1):
        y = y + pltpu.roll(apply(parts, power_ref[...]), shift, 0)
    dressed = v_ref[...] + pltpu.roll(y, 2, 0)
    blocks = [
        dressed[r * SERIES : (r + 1) * SERIES, half * LANES : (half + 1) * LANES] for half in range(2) for r in range(2)
    ]
    green = product(evaluate_ref[...], right(jnp.concatenate(blocks, axis=1)))
    screen = hat_ref[...]
    half = NE // 2
    gc, gs, sc, ss = green[:half], green[half:], screen[:half], screen[half:]
    edge = lax.broadcasted_iota(jnp.int32, gc.shape, 0) == 0
    cc, s2 = gc * sc, gs * ss
    real = jnp.where(edge, cc, cc - s2)
    imag = jnp.where(edge, s2, gc * ss + gs * sc)
    sigma = product(inverse_ref[...], right(jnp.concatenate([real, imag], axis=0)))
    for block in range(4):
        out_ref[pl.ds(block, NE, stride=4), :] = sigma[:, block * LANES : (block + 1) * LANES]


def assemble_kernel(in_ref, out_hbm, sems):
    copies = [
        pltpu.make_async_copy(in_ref.at[e], out_hbm.at[:, e // 4, :, e % 4], sems.at[e]) for e in range(in_ref.shape[0])
    ]
    for copy in copies:
        copy.start()
    for copy in copies:
        copy.wait()


def assemble(pieces):
    devices, energies = pieces.shape[:2]
    tiles = pl.pallas_call(
        assemble_kernel,
        out_shape=jax.ShapeDtypeStruct((energies, devices // 4, 2, 4, 2, LANES), jnp.float32),
        in_specs=[pl.BlockSpec(memory_space=pltpu.VMEM)],
        out_specs=pl.BlockSpec(memory_space=pltpu.HBM),
        scratch_shapes=[pltpu.SemaphoreType.DMA((devices,))],
        compiler_params=pltpu.CompilerParams(vmem_limit_bytes=VMEM_LIMIT),
    )(pieces)
    return tiles.transpose(0, 1, 3, 4, 2, 5).reshape(energies, 2 * devices, BS)


def call(kernel, outs, in_spaces, scratch=(), flops=0, nbytes=0):
    shapes = [jax.ShapeDtypeStruct(s, d) for s, d in outs]
    spaces = {"v": pltpu.VMEM, "s": pltpu.SMEM, "h": pltpu.HBM}
    return pl.pallas_call(
        kernel,
        out_shape=shapes,
        in_specs=[pl.BlockSpec(memory_space=spaces[c]) for c in in_spaces],
        out_specs=[pl.BlockSpec(memory_space=pltpu.VMEM)] * len(outs),
        scratch_shapes=scratch,
        compiler_params=pltpu.CompilerParams(vmem_limit_bytes=VMEM_LIMIT),
        cost_estimate=pl.CostEstimate(flops=flops, bytes_accessed=nbytes, transcendentals=0),
    )


def powers(h, decay, coupling, copies):
    f32 = jnp.float32
    outs = [((copies, 2, RECORD), f32)]
    h, decay, coupling = (pltpu.with_memory_space_constraint(a, pltpu.HBM) for a in (h, decay, coupling))
    scratch = [pltpu.VMEM(s, f32) for s in ((BS, BS), (1, BS), (1, BS))] + [pltpu.SemaphoreType.DMA((3,))]
    return call(powers_kernel, outs, "hhh", scratch, 48 * BS**3, 4 * 2 * BS * BS)(
        h, decay, coupling
    )[0]


def pick(rows, h, screen, forward):
    outs = [((2 * SERIES, BS), jnp.float32), ((NE, WIDE), jnp.float32)] + [((2 * BS, BS), jnp.bfloat16)] * 7
    scratch = [pltpu.VMEM((BS, BS), jnp.float32)] * 2
    return call(picked_kernel, outs, "svvv", scratch, 24 * BS**3, 4 * 12 * BS * BS)(rows, h, screen, forward)


def compose(place, row, copies):
    outs = [((copies, 2, RECORD), jnp.float32), ((2, RECORD), jnp.float32)]
    return call(compose_kernel, outs, "vv", (), 0, 4 * 2 * copies * 2 * RECORD)(place, row)


def convolve(lines, before, series, rights, hat, evaluate, inverse):
    outs = [((4 * NE, LANES), jnp.float32)]
    return call(sigma_kernel, outs, "vvvvvvvvvvvvv", (), 3 * BS**3, 4 * 6 * BS * BS)(
        lines, before, series, *rights, hat, evaluate, inverse
    )[0]


def constants():
    forward, evaluate, inverse = tables()
    def wide(t):
        high = t.astype(ml_dtypes.bfloat16)
        low = (t - high.astype(np.float32)).astype(ml_dtypes.bfloat16)
        return jnp.asarray(np.concatenate([high, low, high], axis=1))
    return wide(forward), wide(evaluate), wide(inverse)


def shards(hamiltonian, decay, coupling, rows, screened):
    forward, evaluate, inverse = constants()
    place = jnp.stack([jnp.full((LANES,), lax.axis_index(name), jnp.int32) for name in ("line", "member")])
    sent = powers(hamiltonian, decay, coupling, lax.axis_size("member"))
    own = 2 * lax.axis_index("energy")
    sent, place, own = lax.optimization_barrier((sent, place, own))
    row = lax.all_to_all(sent, "member", split_axis=0, concat_axis=0, tiled=True)
    row, rows, screened, own = lax.optimization_barrier((row, rows, screened, own))
    mine = lax.dynamic_slice(rows[0], (own,), (2,))
    screen = screened[0].reshape(NE, 2, 2, LANES).transpose(0, 2, 1, 3).reshape(NE, WIDE)
    series, hat, *rights = pick(mine, hamiltonian, screen, forward)
    sent, before = compose(place, row, lax.axis_size("line"))
    lines = lax.all_to_all(sent, "line", split_axis=0, concat_axis=0, tiled=True)
    sigma = convolve(lines, before, series, rights, hat, evaluate, inverse)
    pieces = lax.all_to_all(sigma.reshape(NE, 2, 2, LANES), "energy", split_axis=0, concat_axis=0, tiled=True)
    return assemble(pieces.reshape(lax.axis_size("energy"), -1, 2, 2, LANES))


def solution(mesh):
    energies, slabs = mesh.devices.shape
    fine = Mesh(mesh.devices.reshape(energies, slabs // 8, 8), ("energy", "line", "member"))
    slab = ("line", "member")
    in_specs = (P(slab, None), P(slab, None), P(slab, None), P(slab, None), P(slab, None, "energy", None))
    out_specs = P("energy", slab, None)
    return jax.shard_map(shards, mesh=fine, in_specs=in_specs, out_specs=out_specs, check_vma=False)
```
